32 devices in a mesh: scan: 2 (over x), seq: 16 (over z, y, core).
Axes of the slice: x: 2, y: 2, z: 4, core: 2. Of those that a mesh axis runs over, the one named last changes fastest.
Arguments:
- tokens: bfloat16 [8192, 1024], P(('scan', 'seq')), parts along dimension 0, may hold values from -12 to 12
- ln_gain: float32 [1024], replicated, may hold values from 0.1 to 1.9
- w_query: bfloat16 [1024, 1024], P('seq'), may hold values from -2 to 2
- w_key: bfloat16 [1024, 1024], P('seq'), may hold values from -2 to 2
- w_value: bfloat16 [1024, 1024], P('seq'), may hold values from -0.1875 to 0.1875
- w_out: bfloat16 [1024, 1024], P('seq'), may hold values from -0.1875 to 0.1875
- probe_gain: float32 [1024], replicated, may hold values from 0.1 to 1.9
- probe_queries: bfloat16 [256, 1024], replicated, may hold values from -46 to 46
- key_blocks: int32 [64, 8], P('scan'), parts along dimension 0, may hold values from 0 to 31, as said below
- key_counts: int32 [64], P('scan'), parts along dimension 0, may hold values from 1 to 8, as said below
Outputs:
- layer_out: bfloat16 [8192, 1024], P(('scan', 'seq')), parts along dimension 0
- probe_out: float32 [512, 1024], P(('scan', 'seq')), parts along dimension 0
The draws below stay inside these ranges and needn't reach their ends.
There are 2 independent parts, one for each index of `scan`. The reference program is written for one: setup_inputs(seed, part) draws one part's arguments, and reference() takes and returns one part's arrays. A program takes and returns all parts, laid end to end along the dimension named above; an argument that names none is the same for every part. Nothing has to cross between parts.
Inputs may be any that keep to these rules, and one draw needn't show every extreme that they name: `key_blocks`: entry 0 of each query block's list is that block itself; the entries of one list are different blocks. Entries at or after key_counts are ignored. `key_counts`: some block uses all 8 entries in every draw.
All inputs are finite; a program needn't handle non-finite values.
Results may differ from the reference program's by a relative error of at most 0.0061.
Values may be sent and summed in bfloat16 or wider, within the bound.
No kernel may reach another device: no remote copies, remote signals or barrier semaphores. Data moves between devices by JAX's collectives and lax.ppermute only.
A program may use at most 64 MiB of HBM per device.

```python
import math
import jax
import jax.numpy as jnp
from jax import lax

D = 1024
HEADS = 16
HEAD_DIM = 64
PROBES = 256
BLOCK = 128
MAXK = 8
TOKENS = 4096
QB = 32


def draw_key_counts(key, part):
    base = jax.random.randint(key, (QB,), 1, MAXK + 1)
    spot = jax.random.randint(jax.random.fold_in(key, 7), (), 0, QB)
    return base.at[spot].set(MAXK).astype(jnp.int32)


def draw_key_blocks(key, part):
    row_keys = jax.random.split(key, QB)
    orders = jax.vmap(lambda single: jax.random.permutation(single, QB - 1))(row_keys)
    own = jnp.arange(QB, dtype=jnp.int32)
    others = (own[:, None] + 1 + orders[:, :MAXK - 1].astype(jnp.int32)) % QB
    return jnp.concatenate([own[:, None], others], axis=1).astype(jnp.int32)


def draw_tokens(key, part):
    noise = jnp.clip(jax.random.normal(jax.random.fold_in(key, 1), (TOKENS, D), jnp.float32), -6.0, 6.0)
    return noise.astype(jnp.bfloat16)


def projection_draw(key, salt):
    base = jnp.clip(jax.random.normal(jax.random.fold_in(key, salt), (D, D), jnp.float32), -6.0, 6.0) / math.sqrt(D)
    return base.astype(jnp.bfloat16)


def draw_w_query(key, part):
    return projection_draw(key, 21)


def draw_w_key(key, part):
    return projection_draw(key, 22)


def draw_probe_queries(key, part):
    noise = jnp.clip(jax.random.normal(jax.random.fold_in(key, 31), (PROBES, D), jnp.float32), -6.0, 6.0)
    return noise.astype(jnp.bfloat16)


def block_scale(rng, shape, pieces, smallest, high):
    level, own = 1.0, jax.random.fold_in(rng, 6)
    for axis_at, shards_of in pieces:
        heights = jnp.exp(jax.random.uniform(jax.random.fold_in(own, axis_at), (shards_of,), jnp.float32, smallest / len(pieces), high / len(pieces)))
        level = level * jnp.repeat(heights, shape[axis_at] // shards_of).reshape([-1 if axis == axis_at else 1 for axis in range(len(shape))])
    return level


def centred(stream_key, shape, scale, bound, cuts=(), kind=jnp.bfloat16):
    factor_of = block_scale(stream_key, shape, cuts, -0.22, 0.18) if cuts else 1.0
    array = jax.random.normal(stream_key, shape, jnp.float32) * scale * factor_of
    return jnp.minimum(jnp.maximum(array, -bound), bound).astype(kind)


def setup_inputs(seed: int = 0, part: int = 0) -> dict:
    key_of = jax.random.split(jax.random.key(seed), 11)
    part_keys = jax.random.split(jax.random.fold_in(key_of[10], part), 11)
    tokens = draw_tokens(jax.random.fold_in(jax.random.fold_in(key_of[10], part), 71), part)
    ln_gain = jnp.clip(1.0 + 0.18 * jax.random.normal(key_of[1], (D,), jnp.float32), 0.1, 1.9)
    w_query = draw_w_query(jax.random.fold_in(key_of[10], 71), part)
    w_key = draw_w_key(jax.random.fold_in(key_of[10], 71), part)
    w_value = centred(key_of[4], (D, D), D ** -0.5, 0.1875, ((0, 16),))
    w_out = centred(key_of[5], (D, D), D ** -0.5, 0.1875, ((0, 16),))
    probe_gain = jnp.clip(1.0 + 0.18 * jax.random.normal(key_of[6], (D,), jnp.float32), 0.1, 1.9)
    probe_queries = draw_probe_queries(jax.random.fold_in(key_of[10], 71), part)
    key_blocks = draw_key_blocks(jax.random.fold_in(jax.random.fold_in(key_of[10], part), 71), part)
    key_counts = draw_key_counts(jax.random.fold_in(jax.random.fold_in(key_of[10], part), 71), part)
    return {"tokens": tokens, "ln_gain": ln_gain, "w_query": w_query, "w_key": w_key, "w_value": w_value, "w_out": w_out, "probe_gain": probe_gain, "probe_queries": probe_queries, "key_blocks": key_blocks, "key_counts": key_counts}


EPS = 1e-05

def layer_norm(values, gain):
    wide = values.astype(jnp.float32)
    center = wide - lax.optimization_barrier(jnp.mean(wide, axis=-1, keepdims=True))
    spread = lax.optimization_barrier(jnp.mean(center * center, axis=-1, keepdims=True))
    return (center * lax.rsqrt(spread + EPS) * gain.astype(jnp.float32)).astype(jnp.bfloat16)

def reference(tokens, ln_gain, w_query, w_key, w_value, w_out, probe_gain, probe_queries, key_blocks, key_counts):
    scale = 1.0 / math.sqrt(HEAD_DIM)
    normed = layer_norm(tokens, ln_gain)
    query = jnp.dot(normed, w_query, preferred_element_type=jnp.float32).astype(jnp.bfloat16)
    keys = jnp.dot(normed, w_key, preferred_element_type=jnp.float32).astype(jnp.bfloat16)
    values = jnp.dot(normed, w_value, preferred_element_type=jnp.float32).astype(jnp.bfloat16)
    query_blocks = query.reshape(QB, BLOCK, HEADS, HEAD_DIM)
    key_grid = keys.reshape(QB, BLOCK, HEADS, HEAD_DIM)
    value_grid = values.reshape(QB, BLOCK, HEADS, HEAD_DIM)
    slot_of = jnp.arange(MAXK * BLOCK, dtype=jnp.int32) // BLOCK

    def one_block(index):
        block_query = lax.dynamic_index_in_dim(query_blocks, index, 0, keepdims=False)
        listed = lax.dynamic_index_in_dim(key_blocks, index, 0, keepdims=False).astype(jnp.int32)
        count = lax.dynamic_index_in_dim(key_counts, index, 0, keepdims=False)
        block_keys = key_grid[listed].reshape(MAXK * BLOCK, HEADS, HEAD_DIM)
        block_values = value_grid[listed].reshape(MAXK * BLOCK, HEADS, HEAD_DIM)
        scores = jnp.einsum('qhd,khd->hqk', block_query.astype(jnp.float32), block_keys.astype(jnp.float32), precision=lax.Precision.HIGHEST) * scale
        valid = slot_of < count
        scores = jnp.where(valid[None, None, :], scores, -jnp.inf)
        top = lax.optimization_barrier(jnp.max(scores, axis=-1, keepdims=True))
        weights = jnp.exp(scores - top)
        total = lax.optimization_barrier(jnp.sum(weights, axis=-1, keepdims=True))
        rounded = weights.astype(jnp.bfloat16).astype(jnp.float32)
        mixed = jnp.einsum('hqk,khd->hqd', rounded, block_values.astype(jnp.float32), precision=lax.Precision.HIGHEST) / total
        return jnp.transpose(mixed, (1, 0, 2)).reshape(BLOCK, D).astype(jnp.bfloat16)
    attended = lax.map(one_block, jnp.arange(QB, dtype=jnp.int32)).reshape(TOKENS, D)
    layer_out = (tokens.astype(jnp.float32) + jnp.dot(attended, w_out, preferred_element_type=jnp.float32)).astype(jnp.bfloat16)
    pooled = layer_norm(layer_out, probe_gain)
    pooled_heads = jnp.transpose(pooled.reshape(TOKENS, HEADS, HEAD_DIM), (1, 0, 2))
    probe_heads = jnp.transpose(probe_queries.reshape(PROBES, HEADS, HEAD_DIM), (1, 0, 2))

    def one_head(pair):
        head_probe, head_pooled = pair
        scores = jnp.dot(head_probe, head_pooled.T, preferred_element_type=jnp.float32) * scale
        top = lax.optimization_barrier(jnp.max(scores, axis=-1, keepdims=True))
        weights = jnp.exp(scores - top)
        total = lax.optimization_barrier(jnp.sum(weights, axis=-1, keepdims=True))
        return jnp.dot(weights, head_pooled.astype(jnp.float32), precision=lax.Precision.HIGHEST) / total
    pooled_out = lax.map(one_head, (probe_heads, pooled_heads))
    probe_out = jnp.transpose(pooled_out, (1, 0, 2)).reshape(PROBES, D)
    return (layer_out, probe_out)
```

```python
import functools
import math

import jax
import jax.numpy as jnp
from jax import lax
from jax.experimental import pallas as pl
from jax.experimental.pallas import tpu as pltpu
from jax.sharding import PartitionSpec as P

D = 1024
HEADS = 16
HEAD_DIM = 64
PROBES = 256
BLOCK = 128
MAXK = 8
TOK_DEV = 256
STATS = 128
EPS = 1e-05
SCALE = 1.0 / math.sqrt(HEAD_DIM)
EXP2_SCALE = SCALE / math.log(2.0)
BF16 = jnp.bfloat16
F32 = jnp.float32
NT = (((1,), (1,)), ((), ()))
VMEM_BYTES = 40 * 1024 * 1024


def whole():
    return pl.BlockSpec(memory_space=pltpu.VMEM)


def scalars():
    return pl.BlockSpec(memory_space=pltpu.SMEM)


def params():
    return pltpu.CompilerParams(vmem_limit_bytes=VMEM_BYTES)


def layer_norm(values, gain):
    wide = values.astype(F32)
    center = wide - jnp.mean(wide, axis=-1, keepdims=True)
    spread = jnp.mean(center * center, axis=-1, keepdims=True)
    return (center * lax.rsqrt(spread + EPS) * gain).astype(BF16)


def head_masked(block, heads):
    if heads == 1:
        return block
    lanes = lax.broadcasted_iota(jnp.int32, block.shape, 1) // HEAD_DIM
    zero = jnp.zeros_like(block)
    return jnp.concatenate([jnp.where(lanes == h, block, zero) for h in range(heads)], axis=0)


def project_kernel(count, width, *refs):
    inputs, (gain_ref, weight_ref, query_ref, pair_ref) = refs[:count], refs[count:]
    at = 0
    for ref in inputs:
        rows = ref.shape[0]
        normed = layer_norm(ref[...], gain_ref[...])
        result = jnp.dot(normed, weight_ref[...], preferred_element_type=F32)
        query_ref[at : at + rows, :] = result[:, :width].astype(BF16)
        pair_ref[at : at + rows, :] = result[:, width:].astype(BF16)
        at += rows


def project(pieces, gain, weight, width):
    rows = sum(p.shape[0] for p in pieces)
    return pl.pallas_call(
        functools.partial(project_kernel, len(pieces), width),
        out_shape=(
            jax.ShapeDtypeStruct((rows, width), BF16),
            jax.ShapeDtypeStruct((rows, 2 * width), BF16),
        ),
        in_specs=[whole()] * (len(pieces) + 2),
        out_specs=(whole(), whole()),
        compiler_params=params(),
        name="project",
    )(*pieces, gain, weight)


def attend_kernel(chips, group, heads, sizes, place_ref, lists_ref, counts_ref, *refs):
    n = len(sizes)
    width = heads * HEAD_DIM
    queries, own, other = refs[:n], refs[n : 2 * n], refs[2 * n : 3 * n]
    outs = refs[3 * n : 3 * n + chips]
    q_all, k_all, vt_all, mixed = refs[3 * n + chips :]
    chip, core, member = place_ref[0], place_ref[1], place_ref[2]
    blocks = TOK_DEV // BLOCK
    piece = TOK_DEV // group
    shard = 0
    for i, size in enumerate(sizes):
        for t in range(size):
            owner = place_ref[3 + shard]
            shard += 1
            for u in range(blocks):
                lo = t * TOK_DEV + u * BLOCK
                q_all[owner * blocks + u] = queries[i][lo : lo + BLOCK, :]
                for ref, side in ((own, core), (other, 1 - core)):
                    block = (owner * 2 + side) * blocks + u
                    pair = ref[i][lo : lo + BLOCK, :]
                    k_all[block] = pair[:, :width]
                    vt_all[block] = jnp.transpose(pair[:, width:].astype(F32)).astype(BF16)
    per_piece = piece // BLOCK

    def one_unit(index, carry):
        step = index // per_piece
        part = index % per_piece
        target = lax.bitwise_xor(chip, step)
        within = member * per_piece + part
        block = (target * 2 + core) * blocks + within
        count = counts_ref[block]
        for used in range(1, MAXK + 1):

            @pl.when(count == used)
            def _(used=used):
                picked = [lists_ref[block, s] for s in range(used)]
                stacked = head_masked(q_all[target * blocks + within], heads)
                keys = jnp.concatenate([k_all[p] for p in picked], axis=0)
                scores = lax.dot_general(keys, stacked, NT, preferred_element_type=F32)
                top = jnp.max(scores, axis=0, keepdims=True)
                weights = jnp.exp2((scores - top) * EXP2_SCALE)
                total = jnp.sum(weights, axis=0, keepdims=True)
                values = jnp.concatenate([vt_all[p] for p in picked], axis=1)
                full = jnp.dot(values, weights.astype(BF16), preferred_element_type=F32)
                full = full / total
                result = jnp.concatenate(
                    [
                        full[h * HEAD_DIM : (h + 1) * HEAD_DIM, h * BLOCK : (h + 1) * BLOCK]
                        for h in range(heads)
                    ],
                    axis=0,
                )
                mixed[index] = jnp.transpose(result).astype(BF16)

        return carry

    lax.fori_loop(0, chips * per_piece, one_unit, 0)
    for k in range(chips):
        for part in range(per_piece):
            outs[k][part * BLOCK : (part + 1) * BLOCK, :] = mixed[k * per_piece + part]


def attend(place, lists, counts, queries, own, other, chips, group, heads):
    sizes = tuple(q.shape[0] // TOK_DEV for q in queries)
    width = heads * HEAD_DIM
    piece = TOK_DEV // group
    blocks = TOK_DEV // BLOCK
    n = len(sizes)
    return pl.pallas_call(
        functools.partial(attend_kernel, chips, group, heads, sizes),
        out_shape=[jax.ShapeDtypeStruct((piece, width), BF16)] * chips,
        in_specs=[scalars()] * 3 + [whole()] * (3 * n),
        out_specs=[whole()] * chips,
        scratch_shapes=[
            pltpu.VMEM((chips * blocks, BLOCK, width), BF16),
            pltpu.VMEM((2 * chips * blocks, BLOCK, width), BF16),
            pltpu.VMEM((2 * chips * blocks, width, BLOCK), BF16),
            pltpu.VMEM((chips * (piece // BLOCK), BLOCK, width), BF16),
        ],
        compiler_params=params(),
        name="attend",
    )(place, lists, counts, *queries, *own, *other)


def tail_kernel(chips, group, heads, split, place_ref, *refs):
    width = heads * HEAD_DIM
    sets = HEADS // heads
    piece = TOK_DEV // group
    got = refs[:chips]
    weight_ref, tokens_ref, gain_ref, probe_ref, layer_ref = refs[chips : chips + 5]
    part_refs, (stage,) = refs[chips + 5 : -1], refs[-1:]
    chip, core = place_ref[0], place_ref[1]
    for k in range(chips):
        source = lax.bitwise_xor(chip, k)
        if group == 1:
            stage[source] = got[k][...]
        else:
            stage[source // group, pl.ds(pl.multiple_of(source % group * piece, piece), piece), :] = got[k][...]
    attended = jnp.concatenate([stage[s] for s in range(sets)], axis=1)
    projected = jnp.dot(attended, weight_ref[...], preferred_element_type=F32)
    layer = (tokens_ref[...].astype(F32) + projected).astype(BF16)
    layer_ref[...] = layer
    pooled = layer_norm(layer, gain_ref[...])
    rows = []

    def emit(lo, value):
        hi = lo + value.shape[1]
        if not split:
            part_refs[0][:, lo:hi] = value.astype(BF16)
            return
        share = PROBES // (2 * chips)
        shaped = value.reshape(chips, 2, share, value.shape[1])
        first, second = shaped[:, 0], shaped[:, 1]
        mine = jnp.where(core == 0, first, second)
        theirs = jnp.where(core == 0, second, first)
        part_refs[0][:, lo:hi] = mine.reshape(chips * share, -1).astype(BF16)
        part_refs[1][:, lo:hi] = theirs.reshape(chips * share, -1).astype(BF16)

    for pair in range(HEADS // 2):
        lo = pair * 2 * HEAD_DIM
        own = pooled[:, lo : lo + 2 * HEAD_DIM]
        stacked = head_masked(probe_ref[:, lo : lo + 2 * HEAD_DIM], 2)
        scores = lax.dot_general(own, stacked, NT, preferred_element_type=F32)
        top = jnp.max(scores, axis=0, keepdims=True)
        weights = jnp.exp2((scores - top) * EXP2_SCALE)
        total = jnp.sum(weights, axis=0, keepdims=True)
        flipped = jnp.transpose(own.astype(F32)).astype(BF16)
        full = jnp.dot(flipped, weights.astype(BF16), preferred_element_type=F32) / total
        result = jnp.concatenate([full[:HEAD_DIM, :PROBES], full[HEAD_DIM:, PROBES:]], axis=0)
        emit(lo, jnp.transpose(result))
        logs = top * SCALE + jnp.log(total)
        rows += [logs[:, :PROBES], logs[:, PROBES:]]
    logs = jnp.concatenate(rows, axis=0)
    high = logs.astype(BF16).astype(F32)
    middle = (logs - high).astype(BF16).astype(F32)
    low = logs - high - middle
    rest = jnp.zeros((STATS - 3 * HEADS, PROBES), F32)
    emit(D, jnp.transpose(jnp.concatenate([high, middle, low, rest], axis=0)))


def tail(place, got, weight, tokens, gain, probes, chips, group, heads, split):
    width = heads * HEAD_DIM
    rows = PROBES // 2 if split else PROBES
    return pl.pallas_call(
        functools.partial(tail_kernel, chips, group, heads, split),
        out_shape=[jax.ShapeDtypeStruct((TOK_DEV, D), BF16)]
        + [jax.ShapeDtypeStruct((rows, D + STATS), BF16)] * (2 if split else 1),
        in_specs=[scalars()] + [whole()] * (chips + 4),
        out_specs=[whole()] * (3 if split else 2),
        scratch_shapes=[pltpu.VMEM((HEADS // heads, TOK_DEV, width), BF16)],
        compiler_params=params(),
        name="tail",
    )(place, *got, weight, tokens, gain, probes)


def read_logs(block):
    pick = lax.broadcasted_iota(jnp.int32, (STATS, STATS), 0)
    head = lax.broadcasted_iota(jnp.int32, (STATS, STATS), 1)
    gather = ((pick < 3 * HEADS) & (pick % HEADS == head)).astype(BF16)
    return jnp.dot(block, gather, preferred_element_type=F32)


def spread_heads(factors):
    row = lax.broadcasted_iota(jnp.int32, (STATS, D), 0)
    lane = lax.broadcasted_iota(jnp.int32, (STATS, D), 1)
    widen = (lane // HEAD_DIM == row).astype(F32)
    return jnp.dot(factors, widen, preferred_element_type=F32, precision=lax.Precision.HIGHEST)


def blend(blocks):
    logs = [read_logs(b[:, D:]) for b in blocks]
    top = functools.reduce(jnp.maximum, logs)
    shares = [jnp.exp(one - top) for one in logs]
    total = functools.reduce(jnp.add, shares)
    rows = blocks[0].shape[0]
    wide = spread_heads(jnp.concatenate([s / total for s in shares], axis=0))
    value = 0.0
    for i, b in enumerate(blocks):
        value = value + wide[i * rows : (i + 1) * rows] * b[:, :D].astype(F32)
    return value, top + jnp.log(total)


def pair_kernel(chips, place_ref, mine_ref, got_ref, *outs_and_stage):
    outs, stage = outs_and_stage[:-1], outs_and_stage[-1]
    value, logs = blend([mine_ref[...], got_ref[...]])
    high = logs.astype(BF16).astype(F32)
    middle = (logs - high).astype(BF16).astype(F32)
    low = logs - high - middle
    rest = jnp.zeros((value.shape[0], STATS - 3 * HEADS), F32)
    packed = jnp.concatenate(
        [value, high[:, :HEADS], middle[:, :HEADS], low[:, :HEADS], rest], axis=1
    ).astype(BF16)
    share = value.shape[0] // chips
    stage[...] = packed.reshape(chips, share, D + STATS)
    for k in range(chips):
        outs[k][...] = stage[lax.bitwise_xor(place_ref[0], k)]


def pair_up(place, mine, got, chips):
    share = mine.shape[0] // chips
    return pl.pallas_call(
        functools.partial(pair_kernel, chips),
        out_shape=[jax.ShapeDtypeStruct((share, D + STATS), BF16)] * chips,
        in_specs=[scalars(), whole(), whole()],
        out_specs=[whole()] * chips,
        scratch_shapes=[pltpu.VMEM((chips, share, D + STATS), BF16)],
        compiler_params=params(),
        name="pair_up",
    )(place, mine, got)


def last_kernel(*refs):
    refs[-1][...] = blend([r[...] for r in refs[:-1]])[0]


def join(parts):
    return pl.pallas_call(
        last_kernel,
        out_shape=jax.ShapeDtypeStruct((parts[0].shape[0], D), F32),
        in_specs=[whole()] * len(parts),
        out_specs=whole(),
        compiler_params=params(),
        name="join",
    )(*parts)


def per_device(
    tokens,
    ln_gain,
    w_query,
    w_key,
    w_value,
    w_out,
    probe_gain,
    probe_queries,
    key_blocks,
    key_counts,
):
    ranks = lax.axis_size("seq")
    chips = ranks // 2
    heads = max(1, HEADS // chips)
    group = max(1, chips // HEADS)
    sets = HEADS // heads
    width = heads * HEAD_DIM
    myself = lax.axis_index("seq")
    chip, core = myself // 2, myself % 2
    order = list(range(0, chips, 2)) + list(range(chips - 1, 0, -2))
    swap = [(i, i ^ 1) for i in range(ranks)]
    same_core = [[2 * c + k for c in range(chips)] for k in range(2)]

    def around(shift):
        return [
            (order[i] * 2 + k, order[(i + shift) % chips] * 2 + k)
            for i in range(chips)
            for k in range(2)
        ]

    def across(k):
        return [(2 * c + q, 2 * (c ^ k) + q) for c in range(chips) for q in range(2)]

    depth = w_query.shape[0]
    cut = jnp.stack([w_query, w_key, w_value]).reshape(3, depth, sets, width)
    cut = jnp.transpose(cut, (2, 1, 0, 3)).reshape(sets, depth, 3 * width)
    if group > 1:
        cut = jnp.repeat(cut, group, axis=0)
    here = lax.all_to_all(
        cut, "seq", split_axis=0, concat_axis=0, tiled=True, axis_index_groups=same_core
    )
    there = lax.ppermute(here, "seq", swap)
    even = jnp.where(core == 0, here, there)
    odd = jnp.where(core == 0, there, here)
    weight = jnp.stack([even, odd], axis=1).reshape(D, 3 * width)
    out_weight = lax.all_gather(w_out, "seq", axis=0, tiled=True)

    gain = ln_gain.reshape(1, D)
    steps = [[tokens]]
    forward = backward = tokens
    for s in range(1, chips // 2):
        forward = lax.ppermute(forward, "seq", around(1))
        backward = lax.ppermute(backward, "seq", around(-1))
        steps.append([forward, backward])
    half = TOK_DEV // 2
    steps.append(
        [
            lax.ppermute(forward[:half], "seq", around(1)),
            lax.ppermute(backward[half:], "seq", around(-1)),
        ]
    )
    queries, own, other = [], [], []
    for pieces in steps:
        query, pair = project(pieces, gain, weight, width)
        queries.append(query)
        own.append(pair)
        other.append(lax.ppermute(pair, "seq", swap))

    position = jnp.array([order.index(c) for c in range(chips)], jnp.int32)[chip]
    offsets = [0]
    for s in range(1, chips // 2):
        offsets += [-s, s]
    offsets.append(chips // 2)
    owners = jnp.array(order, jnp.int32)[(position + jnp.array(offsets, jnp.int32)) % chips]
    place = jnp.concatenate([jnp.stack([chip, core, chip % group]), owners]).astype(jnp.int32)

    attended = attend(place, key_blocks, key_counts, queries, own, other, chips, group, heads)
    got = [attended[0]] + [lax.ppermute(attended[k], "seq", across(k)) for k in range(1, chips)]

    share = PROBES // ranks
    split = share % 16 == 0
    layer_out, *parts = tail(
        place,
        got,
        out_weight,
        tokens,
        probe_gain.reshape(1, D),
        probe_queries,
        chips,
        group,
        heads,
        split,
    )
    if split:
        mine, theirs = parts
        pieces = pair_up(place, mine, lax.ppermute(theirs, "seq", swap), chips)
        joined = [pieces[0]] + [
            lax.ppermute(pieces[k], "seq", across(k)) for k in range(1, chips)
        ]
        return layer_out, join(joined)
    rows = lax.all_to_all(
        parts[0].reshape(ranks, share, D + STATS), "seq", split_axis=0, concat_axis=0, tiled=True
    ).astype(F32)
    logs = rows[:, :, D : D + 3 * HEADS].reshape(ranks, share, 3, HEADS).sum(axis=2)
    factors = jnp.exp(logs - jnp.max(logs, axis=0, keepdims=True))
    factors = factors / jnp.sum(factors, axis=0, keepdims=True)
    probe_out = jnp.sum(jnp.repeat(factors, HEAD_DIM, axis=2) * rows[:, :, :D], axis=0)
    return layer_out, probe_out


def solution(mesh):
    return jax.shard_map(
        per_device,
        mesh=mesh,
        in_specs=(
            P(("scan", "seq"), None),
            P(),
            P("seq", None),
            P("seq", None),
            P("seq", None),
            P("seq", None),
            P(),
            P(),
            P("scan", None),
            P("scan"),
        ),
        out_specs=(P(("scan", "seq"), None), P(("scan", "seq"), None)),
        check_vma=False,
    )
```

```python
import functools
import math

import jax
import jax.numpy as jnp
from jax import lax
from jax.experimental import pallas as pl
from jax.experimental.pallas import tpu as pltpu
from jax.sharding import PartitionSpec as P

D = 1024
HEADS = 16
HEAD_DIM = 64
PROBES = 256
BLOCK = 128
MAXK = 8
TOK_DEV = 256
STATS = 128
CHUNK = 4
EPS = 1e-05
SCALE = 1.0 / math.sqrt(HEAD_DIM)
EXP2_SCALE = SCALE / math.log(2.0)
BF16 = jnp.bfloat16
F32 = jnp.float32
NT = (((1,), (1,)), ((), ()))
VMEM_BYTES = 28 * 1024 * 1024


def whole():
    return pl.BlockSpec(memory_space=pltpu.VMEM)


def scalars():
    return pl.BlockSpec(memory_space=pltpu.SMEM)


def params():
    return pltpu.CompilerParams(vmem_limit_bytes=VMEM_BYTES)


def layer_norm(values, gain):
    wide = values.astype(F32)
    center = wide - jnp.mean(wide, axis=-1, keepdims=True)
    spread = jnp.mean(center * center, axis=-1, keepdims=True)
    return (center * lax.rsqrt(spread + EPS) * gain).astype(BF16)


def head_masked(block, heads):
    if heads == 1:
        return block
    lanes = lax.broadcasted_iota(jnp.int32, block.shape, 1) // HEAD_DIM
    zero = jnp.zeros_like(block)
    return jnp.concatenate([jnp.where(lanes == h, block, zero) for h in range(heads)], axis=0)


def chip_and_core():
    rank = lax.axis_index("seq")
    return lax.shift_right_logical(rank, 1), lax.bitwise_and(rank, 1)


def twin():
    return lax.bitwise_and(lax.axis_index("scan"), 1)


def ring_owners(chip, chips):
    half = lax.shift_right_logical(chip, 1)
    position = jnp.where(lax.bitwise_and(chip, 1) == 1, chips - 1 - half, half)
    offsets = [0]
    for s in range(1, chips // 2):
        offsets += [-s, s]
    offsets.append(chips // 2)
    owners = []
    for offset in offsets:
        spot = lax.rem(position + (offset + chips), chips)
        owners.append(jnp.where(spot < chips // 2, 2 * spot, 2 * (chips - 1 - spot) + 1))
    return owners


def prepare_kernel(
    chips, width, tokens_ref, query_ref, key_ref, value_ref, out_ref, load_ref, cut_ref, rows_ref, sems
):
    chip, _ = chip_and_core()
    mine = twin()
    rows = out_ref.shape[0] // 4
    half = TOK_DEV // 2
    step = half + rows
    copies = []
    for i, ref in enumerate((query_ref, key_ref, value_ref)):
        start = pl.multiple_of(mine * (2 * rows), 2 * rows)
        copies.append((ref.at[pl.ds(start, 2 * rows), :], rows_ref.at[i]))
    for part in range(2):
        start = pl.multiple_of(mine * (2 * rows) + part * rows, rows)
        to = load_ref.at[part * step : part * step + half, :]
        copies.append((tokens_ref.at[part * half : (part + 1) * half, :], to))
        to = load_ref.at[part * step + half : (part + 1) * step, :]
        copies.append((out_ref.at[pl.ds(start, rows), :], to))
    copies = [pltpu.make_async_copy(a, b, sems.at[i]) for i, (a, b) in enumerate(copies)]
    for copy in copies:
        copy.start()
    for copy in copies[:3]:
        copy.wait()
    for k in range(chips):
        lanes = pl.ds(pl.multiple_of(lax.bitwise_xor(chip, k) * width, width), width)
        for i in range(3):
            cut_ref[k, :, i * width : (i + 1) * width] = rows_ref[i, :, lanes]
    for copy in copies[3:]:
        copy.wait()


def prepare(tokens, weights, out_weight, chips, width):
    rows = out_weight.shape[0] // 2
    return pl.pallas_call(
        functools.partial(prepare_kernel, chips, width),
        out_shape=(
            jax.ShapeDtypeStruct((TOK_DEV + rows, D), BF16),
            jax.ShapeDtypeStruct((chips, rows, 3 * width), BF16),
        ),
        in_specs=[pl.BlockSpec(memory_space=pltpu.HBM)] * 5,
        out_specs=(whole(), whole()),
        scratch_shapes=[pltpu.VMEM((3, rows, D), BF16), pltpu.SemaphoreType.DMA((7,))],
        compiler_params=params(),
        name="prepare",
    )(*(pltpu.with_memory_space_constraint(x, pltpu.HBM) for x in (tokens, *weights, out_weight)))


def gather_blocks_kernel(picks, ordered, *refs):
    chip, _ = chip_and_core()
    for at, (i, j) in enumerate(picks):
        refs[-1][lax.bitwise_xor(chip, at) if ordered else at] = refs[i][j]


def gather_blocks(blocks, ordered):
    arrays, picks = [], []
    for array, j in blocks:
        if not any(array is one for one in arrays):
            arrays.append(array)
        picks.append(([array is one for one in arrays].index(True), j))
    return pl.pallas_call(
        functools.partial(gather_blocks_kernel, tuple(picks), ordered),
        out_shape=jax.ShapeDtypeStruct((len(blocks),) + arrays[0].shape[1:], BF16),
        in_specs=[whole()] * len(arrays),
        out_specs=whole(),
        compiler_params=params(),
        name="gather_blocks",
    )(*arrays)


def collect_kernel(places, *refs):
    out_ref = refs[-1]
    rows = out_ref.shape[1] // 2
    for i, at in enumerate(places):
        part = i % 2
        out_ref[i // 2, part * rows : (part + 1) * rows, :] = refs[i][at : at + rows, :]


def collect(pieces, rows):
    places = tuple(at + TOK_DEV // 2 for _, at in pieces)
    return pl.pallas_call(
        functools.partial(collect_kernel, places),
        out_shape=jax.ShapeDtypeStruct((len(pieces) // 2, rows, D), BF16),
        in_specs=[whole()] * len(pieces),
        out_specs=whole(),
        compiler_params=params(),
        name="collect",
    )(*(array for array, _ in pieces))


def pair_rows_kernel(chips, ringed, *refs):
    out_ref = refs[-1]
    mine = twin()
    chip, _ = chip_and_core()
    owners = ring_owners(chip, chips) if ringed else range(chips)
    at = 0
    for own_ref, twin_ref in zip(refs[0:-1:2], refs[1:-1:2]):
        for i in range(own_ref.shape[0]):
            out_ref[owners[at], mine] = own_ref[i]
            out_ref[owners[at], 1 - mine] = twin_ref[i]
            at += 1


def pair_rows(pairs, chips, ringed):
    rows, columns = pairs[0][0].shape[1:]
    flat = [p for pair in pairs for p in pair]
    return pl.pallas_call(
        functools.partial(pair_rows_kernel, chips, ringed),
        out_shape=jax.ShapeDtypeStruct((chips, 2, rows, columns), BF16),
        in_specs=[whole()] * len(flat),
        out_specs=whole(),
        compiler_params=params(),
        name="pair_rows",
    )(*flat)


def weave_kernel(own_ref, other_ref, out_ref):
    _, core = chip_and_core()
    chips, rows, columns = own_ref.shape
    for c in range(chips):
        own, other = own_ref[c], other_ref[c]
        out_ref[2 * c * rows : (2 * c + 1) * rows, :] = jnp.where(core == 0, own, other)
        out_ref[(2 * c + 1) * rows : (2 * c + 2) * rows, :] = jnp.where(core == 0, other, own)


def weave(own, other):
    chips, two, rows, columns = own.shape
    own, other = (x.reshape(chips, two * rows, columns) for x in (own, other))
    return pl.pallas_call(
        weave_kernel,
        out_shape=jax.ShapeDtypeStruct((4 * chips * rows, columns), BF16),
        in_specs=[whole()] * 2,
        out_specs=whole(),
        compiler_params=params(),
        name="weave",
    )(own, other)


def shard_blocks(owner, core):
    first = (owner * 2 + core) * (TOK_DEV // BLOCK)
    return [first + u for u in range(TOK_DEV // BLOCK)]


def absorb(pair_ref, kv_all, owners, core):
    blocks = TOK_DEV // BLOCK
    for t, owner in enumerate(owners):
        for u, block in enumerate(shard_blocks(owner, core)):
            kv_all[block] = pair_ref[t * blocks + u]


def project_kernel(chips, starts, width, shards, before, *refs):
    n = len(starts)
    inputs, (gain_ref, weight_ref), (q_all, kv_all, pair_ref) = refs[:n], refs[n : n + 2], refs[-3:]
    chip, core = chip_and_core()
    owners = ring_owners(chip, chips)
    places = [(ref, at) for ref, spots in zip(inputs, starts) for at in spots]
    for begin in range(0, len(places), CHUNK):
        segments = [ref[at : at + BLOCK, :] for ref, at in places[begin : begin + CHUNK]]
        normed = layer_norm(jnp.concatenate(segments, axis=0), gain_ref[...])
        result = jnp.dot(normed, weight_ref[...], preferred_element_type=F32)
        for j in range(len(segments)):
            i = begin + j
            rows = result[j * BLOCK : (j + 1) * BLOCK]
            t, u = divmod(i, TOK_DEV // BLOCK)
            q_all[owners[shards[t]] * (TOK_DEV // BLOCK) + u] = rows[:, :width].astype(BF16)
            pair_ref[i, 0, :, :width] = rows[:, width : 2 * width].astype(BF16)
            pair_ref[i, 1, :width, :] = jnp.transpose(rows[:, 2 * width :]).astype(BF16)
            if width < BLOCK:
                pair_ref[i, 0, :, width:] = jnp.zeros((BLOCK, BLOCK - width), BF16)
                pair_ref[i, 1, width:, :] = jnp.zeros((BLOCK - width, BLOCK), BF16)
    absorb(pair_ref, kv_all, [owners[s] for s in shards], core)
    for i, held in enumerate(before):
        absorb(refs[n + 4 + i], kv_all, [owners[s] for s in held], 1 - core)


def project(pieces, starts, gain, weight, width, chips, shards, before, state):
    blocks = sum(len(s) for s in starts)
    n = len(pieces)
    total = chips * (TOK_DEV // BLOCK)
    return pl.pallas_call(
        functools.partial(project_kernel, chips, starts, width, shards, before),
        out_shape=(
            jax.ShapeDtypeStruct((total, BLOCK, width), BF16),
            jax.ShapeDtypeStruct((2 * total, 2, BLOCK, BLOCK), BF16),
            jax.ShapeDtypeStruct((blocks, 2, BLOCK, BLOCK), BF16),
        ),
        in_specs=[whole()] * (n + 2 + len(state)),
        out_specs=(whole(),) * 3,
        input_output_aliases={n + 2: 0, n + 3: 1} if state else {},
        compiler_params=params(),
        name="project",
    )(*pieces, gain, weight, *state)


def attend_kernel(chips, group, heads, steps, last, lists_ref, counts_ref, q_all, *refs):
    width = heads * HEAD_DIM
    outs, mixed = refs[-1 - len(steps) : -1], refs[-1]
    chip, core = chip_and_core()
    kv_all = refs[0]
    if last:
        kv_all = refs[1 + len(last)]
        owners = ring_owners(chip, chips)
        for i, held in enumerate(last):
            absorb(refs[1 + i], kv_all, [owners[s] for s in held], 1 - core)
    member = lax.rem(chip, group)
    blocks = TOK_DEV // BLOCK
    per_piece = blocks // group

    def place_of(index):
        target = lax.bitwise_xor(chip, steps[0] + lax.div(index, per_piece))
        within = member * per_piece + lax.rem(index, per_piece)
        return target * blocks + within, (target * 2 + core) * blocks + within

    def attend_block(index, used):
        row, block = place_of(index)
        count = counts_ref[block]
        picked = [lists_ref[block, s] for s in range(used)]
        stacked = head_masked(q_all[row], heads)
        scores = []
        for s, p in enumerate(picked):
            one = lax.dot_general(
                kv_all[p, 0][:, :width], stacked, NT, preferred_element_type=F32
            )
            if s:
                one = one + jnp.where(s < count, 0.0, -jnp.inf).astype(F32)
            scores.append(one)
        scores = jnp.concatenate(scores, axis=0)
        top = jnp.max(scores, axis=0, keepdims=True)
        weights = jnp.exp2((scores - top) * EXP2_SCALE)
        total = jnp.sum(weights, axis=0, keepdims=True)
        values = jnp.concatenate([kv_all[p, 1] for p in picked], axis=1)[:width]
        full = jnp.dot(values, weights.astype(BF16), preferred_element_type=F32)
        full = full * (1.0 / total)
        result = jnp.concatenate(
            [
                full[h * HEAD_DIM : (h + 1) * HEAD_DIM, h * BLOCK : (h + 1) * BLOCK]
                for h in range(heads)
            ],
            axis=0,
        )
        return jnp.transpose(result).astype(BF16)

    def one_pair(pair, carry):
        first, second = 2 * pair, 2 * pair + 1
        most = jnp.maximum(counts_ref[place_of(first)[1]], counts_ref[place_of(second)[1]])
        for used in range(1, MAXK + 1):

            @pl.when(most == used)
            def _(used=used):
                one, two = attend_block(first, used), attend_block(second, used)
                mixed[first] = one
                mixed[second] = two

        return carry

    lax.fori_loop(0, len(steps) * per_piece // 2, one_pair, 0)
    for k in range(len(steps)):
        for part in range(per_piece):
            outs[k][part * BLOCK : (part + 1) * BLOCK, :] = mixed[k * per_piece + part]


def attend(lists, counts, q_all, kv_all, extra, chips, group, heads, steps, last):
    width = heads * HEAD_DIM
    piece = TOK_DEV // group
    kv_shape = [jax.ShapeDtypeStruct(kv_all.shape, BF16)] if last else []
    return pl.pallas_call(
        functools.partial(attend_kernel, chips, group, heads, steps, last),
        out_shape=kv_shape + [jax.ShapeDtypeStruct((piece, width), BF16)] * len(steps),
        in_specs=[scalars()] * 2 + [whole()] * (2 + len(extra)),
        out_specs=[whole()] * (len(kv_shape) + len(steps)),
        input_output_aliases={3: 0} if last else {},
        scratch_shapes=[pltpu.VMEM((len(steps) * (piece // BLOCK), BLOCK, width), BF16)],
        compiler_params=params(),
        name="attend",
    )(lists, counts, q_all, kv_all, *extra)


def tail_kernel(chips, group, heads, split, *refs):
    width = heads * HEAD_DIM
    sets = HEADS // heads
    piece = TOK_DEV // group
    got = refs[:chips]
    weight_ref, tokens_ref, gain_ref, probe_ref, layer_ref = refs[chips : chips + 5]
    part_refs, (stage,) = refs[chips + 5 : -1], refs[-1:]
    chip, core = chip_and_core()
    for k in range(chips):
        source = lax.bitwise_xor(chip, k)
        if group == 1:
            stage[source] = got[k][...]
        else:
            stage[source // group, pl.ds(pl.multiple_of(source % group * piece, piece), piece), :] = got[k][...]
    attended = jnp.concatenate([stage[s] for s in range(sets)], axis=1)
    projected = jnp.dot(attended, weight_ref[...], preferred_element_type=F32)
    layer = (tokens_ref[...].astype(F32) + projected).astype(BF16)
    layer_ref[...] = layer
    pooled = layer_norm(layer, gain_ref[...])
    rows = []

    def emit(lo, value):
        hi = lo + value.shape[1]
        if not split:
            part_refs[0][:, lo:hi] = value.astype(BF16)
            return
        share = PROBES // (2 * chips)
        shaped = value.reshape(chips, 2, share, value.shape[1])
        first, second = shaped[:, 0], shaped[:, 1]
        mine = jnp.where(core == 0, first, second)
        theirs = jnp.where(core == 0, second, first)
        part_refs[0][:, lo:hi] = mine.reshape(chips * share, -1).astype(BF16)
        part_refs[1][:, lo:hi] = theirs.reshape(chips * share, -1).astype(BF16)

    for pair in range(HEADS // 2):
        lo = pair * 2 * HEAD_DIM
        own = pooled[:, lo : lo + 2 * HEAD_DIM]
        stacked = head_masked(probe_ref[:, lo : lo + 2 * HEAD_DIM], 2)
        scores = lax.dot_general(own, stacked, NT, preferred_element_type=F32)
        top = jnp.max(scores, axis=0, keepdims=True)
        weights = jnp.exp2((scores - top) * EXP2_SCALE)
        total = jnp.sum(weights, axis=0, keepdims=True)
        flipped = jnp.transpose(own.astype(F32)).astype(BF16)
        full = jnp.dot(flipped, weights.astype(BF16), preferred_element_type=F32) / total
        result = jnp.concatenate([full[:HEAD_DIM, :PROBES], full[HEAD_DIM:, PROBES:]], axis=0)
        emit(lo, jnp.transpose(result))
        logs = top * SCALE + jnp.log(total)
        rows += [logs[:, :PROBES], logs[:, PROBES:]]
    logs = jnp.concatenate(rows, axis=0)
    high = logs.astype(BF16).astype(F32)
    middle = (logs - high).astype(BF16).astype(F32)
    low = logs - high - middle
    rest = jnp.zeros((STATS - 3 * HEADS, PROBES), F32)
    emit(D, jnp.transpose(jnp.concatenate([high, middle, low, rest], axis=0)))


def tail(got, weight, tokens, gain, probes, chips, group, heads, split):
    width = heads * HEAD_DIM
    rows = PROBES // 2 if split else PROBES
    return pl.pallas_call(
        functools.partial(tail_kernel, chips, group, heads, split),
        out_shape=[jax.ShapeDtypeStruct((TOK_DEV, D), BF16)]
        + [jax.ShapeDtypeStruct((rows, D + STATS), BF16)] * (2 if split else 1),
        in_specs=[whole()] * (chips + 4),
        out_specs=[whole()] * (3 if split else 2),
        scratch_shapes=[pltpu.VMEM((HEADS // heads, TOK_DEV, width), BF16)],
        compiler_params=params(),
        name="tail",
    )(*got, weight, tokens, gain, probes)


def read_logs(block):
    pick = lax.broadcasted_iota(jnp.int32, (STATS, STATS), 0)
    head = lax.broadcasted_iota(jnp.int32, (STATS, STATS), 1)
    gather = ((pick < 3 * HEADS) & (pick % HEADS == head)).astype(BF16)
    return jnp.dot(block, gather, preferred_element_type=F32)


def spread_heads(factors):
    row = lax.broadcasted_iota(jnp.int32, (STATS, D), 0)
    lane = lax.broadcasted_iota(jnp.int32, (STATS, D), 1)
    widen = (lane // HEAD_DIM == row).astype(F32)
    return jnp.dot(factors, widen, preferred_element_type=F32, precision=lax.Precision.HIGHEST)


def blend(blocks):
    logs = [read_logs(b[:, D:]) for b in blocks]
    top = functools.reduce(jnp.maximum, logs)
    shares = [jnp.exp(one - top) for one in logs]
    total = functools.reduce(jnp.add, shares)
    rows = blocks[0].shape[0]
    wide = spread_heads(jnp.concatenate([s / total for s in shares], axis=0))
    value = 0.0
    for i, b in enumerate(blocks):
        value = value + wide[i * rows : (i + 1) * rows] * b[:, :D].astype(F32)
    return value, top + jnp.log(total)


def repack(value, logs):
    high = logs.astype(BF16).astype(F32)
    middle = (logs - high).astype(BF16).astype(F32)
    low = logs - high - middle
    rest = jnp.zeros((value.shape[0], STATS - 3 * HEADS), F32)
    return jnp.concatenate(
        [value, high[:, :HEADS], middle[:, :HEADS], low[:, :HEADS], rest], axis=1
    ).astype(BF16)


def deal_kernel(mine_ref, got_ref, *outs_and_stage):
    outs, stage = outs_and_stage[:-1], outs_and_stage[-1]
    chip, _ = chip_and_core()
    packed = repack(*blend([mine_ref[...], got_ref[...]]))
    stage[...] = packed.reshape(stage.shape)
    for k in range(len(outs)):
        outs[k][...] = stage[lax.bitwise_xor(chip, k)]


def deal(mine, got, parts):
    share = mine.shape[0] // parts
    return pl.pallas_call(
        deal_kernel,
        out_shape=[jax.ShapeDtypeStruct((share, D + STATS), BF16)] * parts,
        in_specs=[whole(), whole()],
        out_specs=[whole()] * parts,
        scratch_shapes=[pltpu.VMEM((parts, share, D + STATS), BF16)],
        compiler_params=params(),
        name="deal",
    )(mine, got)


def last_kernel(*refs):
    refs[-1][...] = blend([r[...] for r in refs[:-1]])[0]


def join(parts):
    return pl.pallas_call(
        last_kernel,
        out_shape=jax.ShapeDtypeStruct((parts[0].shape[0], D), F32),
        in_specs=[whole()] * len(parts),
        out_specs=whole(),
        compiler_params=params(),
        name="join",
    )(*parts)


def per_device(
    tokens,
    ln_gain,
    w_query,
    w_key,
    w_value,
    w_out,
    probe_gain,
    probe_queries,
    key_blocks,
    key_counts,
):
    ranks = lax.axis_size("seq")
    chips = ranks // 2
    heads = max(1, HEADS // chips)
    group = max(1, chips // HEADS)
    sets = HEADS // heads
    width = heads * HEAD_DIM
    myself = lax.axis_index("seq")
    core = myself % 2
    order = list(range(0, chips, 2)) + list(range(chips - 1, 0, -2))
    swap = [(i, i ^ 1) for i in range(ranks)]
    same_core = [[2 * c + k for c in range(chips)] for k in range(2)]

    def around(shift):
        return [
            (order[i] * 2 + k, order[(i + shift) % chips] * 2 + k)
            for i in range(chips)
            for k in range(2)
        ]

    def across(k):
        return [(2 * c + q, 2 * (c ^ k) + q) for c in range(chips) for q in range(2)]

    twins = [(i, i ^ 1) for i in range(lax.axis_size("scan"))]
    barrier = lax.optimization_barrier
    depth = w_query.shape[0]
    gain = ln_gain.reshape(1, D)
    half = TOK_DEV // 2
    packed = depth % 64 == 0

    if packed:
        load, parted = prepare(tokens, (w_query, w_key, w_value), w_out, chips, width)
        line = range(chips // 2)
        away = lax.ppermute(
            gather_blocks([(parted, k) for k in range(1, chips, 2)], False), "seq", across(1)
        )
        moved = [
            lax.ppermute(
                gather_blocks([(parted, 2 * k), (away, k)], False), "seq", across(2 * k)
            )
            for k in line[1:]
        ]
    else:
        columns = jnp.stack([w_query, w_key, w_value]).reshape(3, depth, sets, width)
        columns = jnp.transpose(columns, (2, 1, 0, 3)).reshape(sets, depth, 3 * width)
        columns = jnp.repeat(columns, group, axis=0)
        here = lax.all_to_all(
            columns, "seq", split_axis=0, concat_axis=0, tiled=True, axis_index_groups=same_core
        )
        there = lax.ppermute(here, "seq", swap)
        even = jnp.where(core == 0, here, there)
        odd = jnp.where(core == 0, there, here)
        weight = jnp.stack([even, odd], axis=1).reshape(D, 3 * width)
        out_weight = lax.all_gather(w_out, "seq", axis=0, tiled=True)

    load = load if packed else tokens
    length = load.shape[0] // 2
    if packed:
        load, away = barrier((load, away))
    forward = backward = load

    def spread(*shards):
        return [(shard, at) for shard in shards for at in (0, length)]

    state, others = (), []

    def advance(pieces, shards):
        nonlocal state, others
        q_all, kv_all, pair = project(
            [array for array, _ in pieces],
            tuple((at,) for _, at in pieces),
            gain,
            weight,
            width,
            chips,
            shards,
            tuple(held for _, held in others),
            state + tuple(other for other, _ in others),
        )
        state, others = (q_all, kv_all), []
        return pair

    def send(pair, shards):
        others.append((lax.ppermute(pair, "seq", swap), shards))

    arrived, shards = spread(load), (0,)
    for s in range(1, chips // 2 - 1):
        forward = lax.ppermute(forward, "seq", around(1))
        backward = lax.ppermute(backward, "seq", around(-1))
        if packed and s == 1:
            forward, backward, moved[0] = barrier((forward, backward, moved[0]))
        if packed and s == 2:
            sources = [(parted, 0), (away, 0)] + [(m, j) for m in moved for j in range(2)]
            quarter = gather_blocks(sources, True)
            own_half = pair_rows([(quarter, lax.ppermute(quarter, "scan", twins))], chips, False)
            weight = weave(own_half, lax.ppermute(own_half, "seq", swap))
            forward, backward, weight = barrier((forward, backward, weight))
        arrived += spread(forward, backward)
        shards += (2 * s - 1, 2 * s)
    if packed:
        early = collect(arrived, depth // 2)
        early_twin = lax.ppermute(early, "scan", twins)
        weight, early_twin = barrier((weight, early_twin))
    pair = advance(arrived, shards)
    forward = lax.ppermute(forward, "seq", around(1))
    backward = lax.ppermute(backward, "seq", around(-1))
    forward, backward, pair, *state = barrier((forward, backward, pair, *state))
    state = tuple(state)
    final = (
        lax.ppermute(forward[:length], "seq", around(1)),
        lax.ppermute(backward[length:], "seq", around(-1)),
    )
    pair, *final = barrier((pair, *final))
    send(pair, shards)
    held, others = others, []
    last = spread(forward, backward) + [(array, 0) for array in final]
    last_shards = (chips - 3, chips - 2, chips - 1)
    send(advance(last, last_shards), last_shards)
    others = held + others
    if packed:
        middle = collect(spread(forward, backward), depth // 2)
        middle_twin = lax.ppermute(middle, "scan", twins)
        late = collect(last[-2:], depth // 2)
        late_twin = lax.ppermute(late, "scan", twins)
    q_all, kv_all = state
    far = tuple(range(chips // 2, chips))
    near = tuple(range(chips // 2))
    kv_all, *first = attend(
        key_blocks,
        key_counts,
        q_all,
        kv_all,
        [other for other, _ in others],
        chips,
        group,
        heads,
        far,
        tuple(held for _, held in others),
    )
    if packed:
        kv_all, middle_twin, late_twin = barrier((kv_all, middle_twin, late_twin))
        own_half = pair_rows(
            [(early, early_twin), (middle, middle_twin), (late, late_twin)], chips, True
        )
        other_half = lax.ppermute(own_half, "seq", swap)
    sent = [lax.ppermute(first[i], "seq", across(k)) for i, k in enumerate(far)]
    second = attend(key_blocks, key_counts, q_all, kv_all, (), chips, group, heads, near, ())
    got = [second[0]] + [lax.ppermute(second[k], "seq", across(k)) for k in near[1:]] + sent
    if packed:
        out_weight = weave(own_half, other_half)

    share = PROBES // ranks
    split = share % 16 == 0
    layer_out, *parts = tail(
        got,
        out_weight,
        tokens,
        probe_gain.reshape(1, D),
        probe_queries,
        chips,
        group,
        heads,
        split,
    )
    if split:
        mine, theirs = parts
        blocks = deal(mine, lax.ppermute(theirs, "seq", swap), chips)
        joined = [blocks[0]] + [
            lax.ppermute(blocks[k], "seq", across(k)) for k in range(1, chips)
        ]
        return layer_out, join(joined)
    rows = lax.all_to_all(
        parts[0].reshape(ranks, share, D + STATS), "seq", split_axis=0, concat_axis=0, tiled=True
    ).astype(F32)
    logs = rows[:, :, D : D + 3 * HEADS].reshape(ranks, share, 3, HEADS).sum(axis=2)
    factors = jnp.exp(logs - jnp.max(logs, axis=0, keepdims=True))
    factors = factors / jnp.sum(factors, axis=0, keepdims=True)
    probe_out = jnp.sum(jnp.repeat(factors, HEAD_DIM, axis=2) * rows[:, :, :D], axis=0)
    return layer_out, probe_out


def solution(mesh):
    return jax.shard_map(
        per_device,
        mesh=mesh,
        in_specs=(
            P(("scan", "seq"), None),
            P(),
            P("seq", None),
            P("seq", None),
            P("seq", None),
            P("seq", None),
            P(),
            P(),
            P("scan", None),
            P("scan"),
        ),
        out_specs=(P(("scan", "seq"), None), P(("scan", "seq"), None)),
        check_vma=False,
    )
```

```python
import functools
import math

import jax
import jax.numpy as jnp
from jax import lax
from jax.experimental import pallas as pl
from jax.experimental.pallas import tpu as pltpu
from jax.sharding import PartitionSpec as P

D = 1024
HEADS = 16
HEAD_DIM = 64
PROBES = 256
BLOCK = 128
MAXK = 8
TOK_DEV = 256
STATS = 128
CHUNK = 4
EPS = 1e-05
SCALE = 1.0 / math.sqrt(HEAD_DIM)
EXP2_SCALE = SCALE / math.log(2.0)
BF16 = jnp.bfloat16
F32 = jnp.float32
NT = (((1,), (1,)), ((), ()))
VMEM_BYTES = 28 * 1024 * 1024


def whole():
    return pl.BlockSpec(memory_space=pltpu.VMEM)


def scalars():
    return pl.BlockSpec(memory_space=pltpu.SMEM)


def params():
    return pltpu.CompilerParams(vmem_limit_bytes=VMEM_BYTES)


def layer_norm(values, gain):
    wide = values.astype(F32)
    center = wide - jnp.mean(wide, axis=-1, keepdims=True)
    spread = jnp.mean(center * center, axis=-1, keepdims=True)
    return (center * lax.rsqrt(spread + EPS) * gain).astype(BF16)


def head_masked(block, heads):
    if heads == 1:
        return block
    lanes = lax.broadcasted_iota(jnp.int32, block.shape, 1) // HEAD_DIM
    zero = jnp.zeros_like(block)
    return jnp.concatenate([jnp.where(lanes == h, block, zero) for h in range(heads)], axis=0)


def chip_and_core():
    rank = lax.axis_index("seq")
    return lax.shift_right_logical(rank, 1), lax.bitwise_and(rank, 1)


def twin():
    return lax.bitwise_and(lax.axis_index("scan"), 1)


def ring_owners(chip, chips):
    half = lax.shift_right_logical(chip, 1)
    position = jnp.where(lax.bitwise_and(chip, 1) == 1, chips - 1 - half, half)
    offsets = [0]
    for s in range(1, chips // 2):
        offsets += [-s, s]
    offsets.append(chips // 2)
    owners = []
    for offset in offsets:
        spot = lax.rem(position + (offset + chips), chips)
        owners.append(jnp.where(spot < chips // 2, 2 * spot, 2 * (chips - 1 - spot) + 1))
    return owners


def prepare_kernel(
    chips, width, tokens_ref, query_ref, key_ref, value_ref, out_ref, load_ref, cut_ref, rows_ref, sems
):
    chip, _ = chip_and_core()
    mine = twin()
    rows = out_ref.shape[0] // 4
    half = TOK_DEV // 2
    step = half + rows
    copies = []
    for i, ref in enumerate((query_ref, key_ref, value_ref)):
        start = pl.multiple_of(mine * (2 * rows), 2 * rows)
        copies.append((ref.at[pl.ds(start, 2 * rows), :], rows_ref.at[i]))
    for part in range(2):
        start = pl.multiple_of(mine * (2 * rows) + part * rows, rows)
        to = load_ref.at[part * step : part * step + half, :]
        copies.append((tokens_ref.at[part * half : (part + 1) * half, :], to))
        to = load_ref.at[part * step + half : (part + 1) * step, :]
        copies.append((out_ref.at[pl.ds(start, rows), :], to))
    copies = [pltpu.make_async_copy(a, b, sems.at[i]) for i, (a, b) in enumerate(copies)]
    for copy in copies:
        copy.start()
    for copy in copies[:3]:
        copy.wait()
    for k in range(chips):
        lanes = pl.ds(pl.multiple_of(lax.bitwise_xor(chip, k) * width, width), width)
        for i in range(3):
            cut_ref[k, :, i * width : (i + 1) * width] = rows_ref[i, :, lanes]
    for copy in copies[3:]:
        copy.wait()


def prepare(tokens, weights, out_weight, chips, width):
    rows = out_weight.shape[0] // 2
    return pl.pallas_call(
        functools.partial(prepare_kernel, chips, width),
        out_shape=(
            jax.ShapeDtypeStruct((TOK_DEV + rows, D), BF16),
            jax.ShapeDtypeStruct((chips, rows, 3 * width), BF16),
        ),
        in_specs=[pl.BlockSpec(memory_space=pltpu.HBM)] * 5,
        out_specs=(whole(), whole()),
        scratch_shapes=[pltpu.VMEM((3, rows, D), BF16), pltpu.SemaphoreType.DMA((7,))],
        compiler_params=params(),
        name="prepare",
    )(*(pltpu.with_memory_space_constraint(x, pltpu.HBM) for x in (tokens, *weights, out_weight)))


def gather_blocks_kernel(picks, ordered, *refs):
    chip, _ = chip_and_core()
    for at, (i, j) in enumerate(picks):
        refs[-1][lax.bitwise_xor(chip, at) if ordered else at] = refs[i][j]


def gather_blocks(blocks, ordered):
    arrays, picks = [], []
    for array, j in blocks:
        if not any(array is one for one in arrays):
            arrays.append(array)
        picks.append(([array is one for one in arrays].index(True), j))
    return pl.pallas_call(
        functools.partial(gather_blocks_kernel, tuple(picks), ordered),
        out_shape=jax.ShapeDtypeStruct((len(blocks),) + arrays[0].shape[1:], BF16),
        in_specs=[whole()] * len(arrays),
        out_specs=whole(),
        compiler_params=params(),
        name="gather_blocks",
    )(*arrays)


def collect_kernel(places, *refs):
    out_ref = refs[-1]
    rows = out_ref.shape[1] // 2
    for i, at in enumerate(places):
        part = i % 2
        out_ref[i // 2, part * rows : (part + 1) * rows, :] = refs[i][at : at + rows, :]


def collect(pieces, rows):
    places = tuple(at + TOK_DEV // 2 for _, at in pieces)
    return pl.pallas_call(
        functools.partial(collect_kernel, places),
        out_shape=jax.ShapeDtypeStruct((len(pieces) // 2, rows, D), BF16),
        in_specs=[whole()] * len(pieces),
        out_specs=whole(),
        compiler_params=params(),
        name="collect",
    )(*(array for array, _ in pieces))


def pair_rows_kernel(chips, ringed, *refs):
    out_ref = refs[-1]
    mine = twin()
    chip, _ = chip_and_core()
    owners = ring_owners(chip, chips) if ringed else range(chips)
    at = 0
    for own_ref, twin_ref in zip(refs[0:-1:2], refs[1:-1:2]):
        for i in range(own_ref.shape[0]):
            out_ref[owners[at], mine] = own_ref[i]
            out_ref[owners[at], 1 - mine] = twin_ref[i]
            at += 1


def pair_rows(pairs, chips, ringed):
    rows, columns = pairs[0][0].shape[1:]
    flat = [p for pair in pairs for p in pair]
    return pl.pallas_call(
        functools.partial(pair_rows_kernel, chips, ringed),
        out_shape=jax.ShapeDtypeStruct((chips, 2, rows, columns), BF16),
        in_specs=[whole()] * len(flat),
        out_specs=whole(),
        compiler_params=params(),
        name="pair_rows",
    )(*flat)


def weave_kernel(own_ref, other_ref, out_ref):
    _, core = chip_and_core()
    chips, rows, columns = own_ref.shape
    for c in range(chips):
        own, other = own_ref[c], other_ref[c]
        out_ref[2 * c * rows : (2 * c + 1) * rows, :] = jnp.where(core == 0, own, other)
        out_ref[(2 * c + 1) * rows : (2 * c + 2) * rows, :] = jnp.where(core == 0, other, own)


def weave(own, other):
    chips, two, rows, columns = own.shape
    own, other = (x.reshape(chips, two * rows, columns) for x in (own, other))
    return pl.pallas_call(
        weave_kernel,
        out_shape=jax.ShapeDtypeStruct((4 * chips * rows, columns), BF16),
        in_specs=[whole()] * 2,
        out_specs=whole(),
        compiler_params=params(),
        name="weave",
    )(own, other)


def shard_blocks(owner, core):
    first = (owner * 2 + core) * (TOK_DEV // BLOCK)
    return [first + u for u in range(TOK_DEV // BLOCK)]


def absorb(pair_ref, kv_all, owners, core):
    blocks = TOK_DEV // BLOCK
    for t, owner in enumerate(owners):
        for u, block in enumerate(shard_blocks(owner, core)):
            kv_all[block] = pair_ref[t * blocks + u]


def project_kernel(chips, starts, width, shards, before, *refs):
    n = len(starts)
    inputs, (gain_ref, weight_ref), (q_all, kv_all, pair_ref) = refs[:n], refs[n : n + 2], refs[-3:]
    chip, core = chip_and_core()
    owners = ring_owners(chip, chips)
    places = [(ref, at) for ref, spots in zip(inputs, starts) for at in spots]
    for begin in range(0, len(places), CHUNK):
        segments = [ref[at : at + BLOCK, :] for ref, at in places[begin : begin + CHUNK]]
        normed = layer_norm(jnp.concatenate(segments, axis=0), gain_ref[...])
        result = jnp.dot(normed, weight_ref[...], preferred_element_type=F32)
        for j in range(len(segments)):
            i = begin + j
            rows = result[j * BLOCK : (j + 1) * BLOCK]
            t, u = divmod(i, TOK_DEV // BLOCK)
            q_all[owners[shards[t]] * (TOK_DEV // BLOCK) + u] = rows[:, :width].astype(BF16)
            pair_ref[i, 0, :, :width] = rows[:, width : 2 * width].astype(BF16)
            pair_ref[i, 1, :width, :] = jnp.transpose(rows[:, 2 * width :]).astype(BF16)
            if width < BLOCK:
                pair_ref[i, 0, :, width:] = jnp.zeros((BLOCK, BLOCK - width), BF16)
                pair_ref[i, 1, width:, :] = jnp.zeros((BLOCK - width, BLOCK), BF16)
    absorb(pair_ref, kv_all, [owners[s] for s in shards], core)
    for i, held in enumerate(before):
        absorb(refs[n + 4 + i], kv_all, [owners[s] for s in held], 1 - core)


def project(pieces, starts, gain, weight, width, chips, shards, before, state):
    blocks = sum(len(s) for s in starts)
    n = len(pieces)
    total = chips * (TOK_DEV // BLOCK)
    return pl.pallas_call(
        functools.partial(project_kernel, chips, starts, width, shards, before),
        out_shape=(
            jax.ShapeDtypeStruct((total, BLOCK, width), BF16),
            jax.ShapeDtypeStruct((2 * total, 2, BLOCK, BLOCK), BF16),
            jax.ShapeDtypeStruct((blocks, 2, BLOCK, BLOCK), BF16),
        ),
        in_specs=[whole()] * (n + 2 + len(state)),
        out_specs=(whole(),) * 3,
        input_output_aliases={n + 2: 0, n + 3: 1} if state else {},
        compiler_params=params(),
        name="project",
    )(*pieces, gain, weight, *state)


def attend_kernel(chips, group, heads, steps, last, lists_ref, counts_ref, q_all, *refs):
    width = heads * HEAD_DIM
    outs, mixed = refs[-1 - len(steps) : -1], refs[-1]
    chip, core = chip_and_core()
    kv_all = refs[0]
    if last:
        kv_all = refs[1 + len(last)]
        owners = ring_owners(chip, chips)
        for i, held in enumerate(last):
            absorb(refs[1 + i], kv_all, [owners[s] for s in held], 1 - core)
    member = lax.rem(chip, group)
    blocks = TOK_DEV // BLOCK
    per_piece = blocks // group

    def place_of(index):
        target = lax.bitwise_xor(chip, steps[0] + lax.div(index, per_piece))
        within = member * per_piece + lax.rem(index, per_piece)
        return target * blocks + within, (target * 2 + core) * blocks + within

    def attend_block(index, used):
        row, block = place_of(index)
        count = counts_ref[block]
        picked = [lists_ref[block, s] for s in range(used)]
        stacked = head_masked(q_all[row], heads)
        scores = []
        for s, p in enumerate(picked):
            one = lax.dot_general(
                kv_all[p, 0][:, :width], stacked, NT, preferred_element_type=F32
            )
            if s:
                one = one + jnp.where(s < count, 0.0, -jnp.inf).astype(F32)
            scores.append(one)
        scores = jnp.concatenate(scores, axis=0)
        top = jnp.max(scores, axis=0, keepdims=True)
        weights = jnp.exp2((scores - top) * EXP2_SCALE)
        total = jnp.sum(weights, axis=0, keepdims=True)
        values = jnp.concatenate([kv_all[p, 1] for p in picked], axis=1)[:width]
        full = jnp.dot(values, weights.astype(BF16), preferred_element_type=F32)
        full = full * (1.0 / total)
        result = jnp.concatenate(
            [
                full[h * HEAD_DIM : (h + 1) * HEAD_DIM, h * BLOCK : (h + 1) * BLOCK]
                for h in range(heads)
            ],
            axis=0,
        )
        return jnp.transpose(result).astype(BF16)

    def one_pair(pair, carry):
        first, second = 2 * pair, 2 * pair + 1
        most = jnp.maximum(counts_ref[place_of(first)[1]], counts_ref[place_of(second)[1]])
        for used in range(1, MAXK + 1):

            @pl.when(most == used)
            def _(used=used):
                one, two = attend_block(first, used), attend_block(second, used)
                mixed[first] = one
                mixed[second] = two

        return carry

    lax.fori_loop(0, len(steps) * per_piece // 2, one_pair, 0)
    for k in range(len(steps)):
        for part in range(per_piece):
            outs[k][part * BLOCK : (part + 1) * BLOCK, :] = mixed[k * per_piece + part]


def attend(lists, counts, q_all, kv_all, extra, chips, group, heads, steps, last):
    width = heads * HEAD_DIM
    piece = TOK_DEV // group
    kv_shape = [jax.ShapeDtypeStruct(kv_all.shape, BF16)] if last else []
    return pl.pallas_call(
        functools.partial(attend_kernel, chips, group, heads, steps, last),
        out_shape=kv_shape + [jax.ShapeDtypeStruct((piece, width), BF16)] * len(steps),
        in_specs=[scalars()] * 2 + [whole()] * (2 + len(extra)),
        out_specs=[whole()] * (len(kv_shape) + len(steps)),
        input_output_aliases={3: 0} if last else {},
        scratch_shapes=[pltpu.VMEM((len(steps) * (piece // BLOCK), BLOCK, width), BF16)],
        compiler_params=params(),
        name="attend",
    )(lists, counts, q_all, kv_all, *extra)


def tail_kernel(chips, group, heads, split, parts, *refs):
    width = heads * HEAD_DIM
    sets = HEADS // heads
    piece = TOK_DEV // group
    got = refs[:chips]
    tokens_ref, gain_ref, probe_ref, *weight_refs = refs[chips : chips + 3 + parts]
    layer_ref, *part_refs, stage = refs[chips + 3 + parts :]
    chip, core = chip_and_core()
    for k in range(chips):
        source = lax.bitwise_xor(chip, k)
        if group == 1:
            stage[source] = got[k][...]
        else:
            stage[source // group, pl.ds(pl.multiple_of(source % group * piece, piece), piece), :] = got[k][...]
    if parts == 1:
        attended = jnp.concatenate([stage[s] for s in range(sets)], axis=1)
        projected = jnp.dot(attended, weight_refs[0][...], preferred_element_type=F32)
    else:
        left = lax.broadcasted_iota(jnp.int32, (TOK_DEV, width), 1) < HEAD_DIM
        ours, theirs = [], []
        for s in range(0, sets, 2):
            one, two = stage[s], stage[s + 1]
            first = jnp.where(left, one, pltpu.roll(two, HEAD_DIM, axis=1))
            second = jnp.where(left, pltpu.roll(one, HEAD_DIM, axis=1), two)
            ours.append(jnp.where(core == 0, first, second))
            theirs.append(jnp.where(core == 0, second, first))
        projected = jnp.dot(
            jnp.concatenate(ours, axis=1), weight_refs[0][...], preferred_element_type=F32
        )
        projected += jnp.dot(
            jnp.concatenate(theirs, axis=1), weight_refs[1][...], preferred_element_type=F32
        )
    layer = (tokens_ref[...].astype(F32) + projected).astype(BF16)
    layer_ref[...] = layer
    pooled = layer_norm(layer, gain_ref[...])
    rows = []

    def emit(lo, value):
        hi = lo + value.shape[1]
        if not split:
            part_refs[0][:, lo:hi] = value.astype(BF16)
            return
        share = PROBES // (2 * chips)
        shaped = value.reshape(chips, 2, share, value.shape[1])
        first, second = shaped[:, 0], shaped[:, 1]
        mine = jnp.where(core == 0, first, second)
        theirs = jnp.where(core == 0, second, first)
        part_refs[0][:, lo:hi] = mine.reshape(chips * share, -1).astype(BF16)
        part_refs[1][:, lo:hi] = theirs.reshape(chips * share, -1).astype(BF16)

    for pair in range(HEADS // 2):
        lo = pair * 2 * HEAD_DIM
        own = pooled[:, lo : lo + 2 * HEAD_DIM]
        stacked = head_masked(probe_ref[:, lo : lo + 2 * HEAD_DIM], 2)
        scores = lax.dot_general(own, stacked, NT, preferred_element_type=F32)
        top = jnp.max(scores, axis=0, keepdims=True)
        weights = jnp.exp2((scores - top) * EXP2_SCALE)
        total = jnp.sum(weights, axis=0, keepdims=True)
        flipped = jnp.transpose(own.astype(F32)).astype(BF16)
        full = jnp.dot(flipped, weights.astype(BF16), preferred_element_type=F32) / total
        result = jnp.concatenate([full[:HEAD_DIM, :PROBES], full[HEAD_DIM:, PROBES:]], axis=0)
        emit(lo, jnp.transpose(result))
        logs = top * SCALE + jnp.log(total)
        rows += [logs[:, :PROBES], logs[:, PROBES:]]
    logs = jnp.concatenate(rows, axis=0)
    high = logs.astype(BF16).astype(F32)
    middle = (logs - high).astype(BF16).astype(F32)
    low = logs - high - middle
    rest = jnp.zeros((STATS - 3 * HEADS, PROBES), F32)
    emit(D, jnp.transpose(jnp.concatenate([high, middle, low, rest], axis=0)))


def tail(got, weights, tokens, gain, probes, chips, group, heads, split):
    width = heads * HEAD_DIM
    rows = PROBES // 2 if split else PROBES
    return pl.pallas_call(
        functools.partial(tail_kernel, chips, group, heads, split, len(weights)),
        out_shape=[jax.ShapeDtypeStruct((TOK_DEV, D), BF16)]
        + [jax.ShapeDtypeStruct((rows, D + STATS), BF16)] * (2 if split else 1),
        in_specs=[whole()] * (chips + 3 + len(weights)),
        out_specs=[whole()] * (3 if split else 2),
        scratch_shapes=[pltpu.VMEM((HEADS // heads, TOK_DEV, width), BF16)],
        compiler_params=params(),
        name="tail",
    )(*got, tokens, gain, probes, *weights)


def read_logs(block):
    pick = lax.broadcasted_iota(jnp.int32, (STATS, STATS), 0)
    head = lax.broadcasted_iota(jnp.int32, (STATS, STATS), 1)
    gather = ((pick < 3 * HEADS) & (pick % HEADS == head)).astype(BF16)
    return jnp.dot(block, gather, preferred_element_type=F32)


def spread_heads(factors):
    row = lax.broadcasted_iota(jnp.int32, (STATS, D), 0)
    lane = lax.broadcasted_iota(jnp.int32, (STATS, D), 1)
    widen = (lane // HEAD_DIM == row).astype(F32)
    return jnp.dot(factors, widen, preferred_element_type=F32, precision=lax.Precision.HIGHEST)


def blend(blocks):
    logs = [read_logs(b[:, D:]) for b in blocks]
    top = functools.reduce(jnp.maximum, logs)
    shares = [jnp.exp(one - top) for one in logs]
    total = functools.reduce(jnp.add, shares)
    rows = blocks[0].shape[0]
    wide = spread_heads(jnp.concatenate([s / total for s in shares], axis=0))
    value = 0.0
    for i, b in enumerate(blocks):
        value = value + wide[i * rows : (i + 1) * rows] * b[:, :D].astype(F32)
    return value, top + jnp.log(total)


def repack(value, logs):
    high = logs.astype(BF16).astype(F32)
    middle = (logs - high).astype(BF16).astype(F32)
    low = logs - high - middle
    rest = jnp.zeros((value.shape[0], STATS - 3 * HEADS), F32)
    return jnp.concatenate(
        [value, high[:, :HEADS], middle[:, :HEADS], low[:, :HEADS], rest], axis=1
    ).astype(BF16)


def deal_kernel(mine_ref, got_ref, *outs_and_stage):
    outs, stage = outs_and_stage[:-1], outs_and_stage[-1]
    chip, _ = chip_and_core()
    packed = repack(*blend([mine_ref[...], got_ref[...]]))
    stage[...] = packed.reshape(stage.shape)
    for k in range(len(outs)):
        outs[k][...] = stage[lax.bitwise_xor(chip, k)]


def deal(mine, got, parts):
    share = mine.shape[0] // parts
    return pl.pallas_call(
        deal_kernel,
        out_shape=[jax.ShapeDtypeStruct((share, D + STATS), BF16)] * parts,
        in_specs=[whole(), whole()],
        out_specs=[whole()] * parts,
        scratch_shapes=[pltpu.VMEM((parts, share, D + STATS), BF16)],
        compiler_params=params(),
        name="deal",
    )(mine, got)


def last_kernel(*refs):
    refs[-1][...] = blend([r[...] for r in refs[:-1]])[0]


def join(parts):
    return pl.pallas_call(
        last_kernel,
        out_shape=jax.ShapeDtypeStruct((parts[0].shape[0], D), F32),
        in_specs=[whole()] * len(parts),
        out_specs=whole(),
        compiler_params=params(),
        name="join",
    )(*parts)


def per_device(
    tokens,
    ln_gain,
    w_query,
    w_key,
    w_value,
    w_out,
    probe_gain,
    probe_queries,
    key_blocks,
    key_counts,
):
    ranks = lax.axis_size("seq")
    chips = ranks // 2
    heads = max(1, HEADS // chips)
    group = max(1, chips // HEADS)
    sets = HEADS // heads
    width = heads * HEAD_DIM
    myself = lax.axis_index("seq")
    core = myself % 2
    order = list(range(0, chips, 2)) + list(range(chips - 1, 0, -2))
    swap = [(i, i ^ 1) for i in range(ranks)]
    same_core = [[2 * c + k for c in range(chips)] for k in range(2)]

    def around(shift):
        return [
            (order[i] * 2 + k, order[(i + shift) % chips] * 2 + k)
            for i in range(chips)
            for k in range(2)
        ]

    def across(k):
        return [(2 * c + q, 2 * (c ^ k) + q) for c in range(chips) for q in range(2)]

    twins = [(i, i ^ 1) for i in range(lax.axis_size("scan"))]
    barrier = lax.optimization_barrier
    depth = w_query.shape[0]
    gain = ln_gain.reshape(1, D)
    half = TOK_DEV // 2
    packed = depth % 64 == 0

    if packed:
        load, parted = prepare(tokens, (w_query, w_key, w_value), w_out, chips, width)
        line = range(chips // 2)
        away = lax.ppermute(
            gather_blocks([(parted, k) for k in range(1, chips, 2)], False), "seq", across(1)
        )
        moved = [
            lax.ppermute(
                gather_blocks([(parted, 2 * k), (away, k)], False), "seq", across(2 * k)
            )
            for k in line[1:]
        ]
    else:
        columns = jnp.stack([w_query, w_key, w_value]).reshape(3, depth, sets, width)
        columns = jnp.transpose(columns, (2, 1, 0, 3)).reshape(sets, depth, 3 * width)
        columns = jnp.repeat(columns, group, axis=0)
        here = lax.all_to_all(
            columns, "seq", split_axis=0, concat_axis=0, tiled=True, axis_index_groups=same_core
        )
        there = lax.ppermute(here, "seq", swap)
        even = jnp.where(core == 0, here, there)
        odd = jnp.where(core == 0, there, here)
        weight = jnp.stack([even, odd], axis=1).reshape(D, 3 * width)
        out_weights = [lax.all_gather(w_out, "seq", axis=0, tiled=True)]

    load = load if packed else tokens
    length = load.shape[0] // 2
    if packed:
        load, away = barrier((load, away))
    forward = backward = load

    def spread(*shards):
        return [(shard, at) for shard in shards for at in (0, length)]

    state, others = (), []

    def advance(pieces, shards):
        nonlocal state, others
        q_all, kv_all, pair = project(
            [array for array, _ in pieces],
            tuple((at,) for _, at in pieces),
            gain,
            weight,
            width,
            chips,
            shards,
            tuple(held for _, held in others),
            state + tuple(other for other, _ in others),
        )
        state, others = (q_all, kv_all), []
        return pair

    def send(pair, shards):
        others.append((lax.ppermute(pair, "seq", swap), shards))

    arrived, shards = spread(load), (0,)
    for s in range(1, chips // 2 - 1):
        forward = lax.ppermute(forward, "seq", around(1))
        backward = lax.ppermute(backward, "seq", around(-1))
        if packed and s == 1:
            forward, backward, moved[0] = barrier((forward, backward, moved[0]))
        if packed and s == 2:
            sources = [(parted, 0), (away, 0)] + [(m, j) for m in moved for j in range(2)]
            quarter = gather_blocks(sources, True)
            own_half = pair_rows([(quarter, lax.ppermute(quarter, "scan", twins))], chips, False)
            weight = weave(own_half, lax.ppermute(own_half, "seq", swap))
            forward, backward, weight = barrier((forward, backward, weight))
        arrived += spread(forward, backward)
        shards += (2 * s - 1, 2 * s)
    if packed:
        early = collect(arrived, depth // 2)
        early_twin = lax.ppermute(early, "scan", twins)
        weight, early_twin = barrier((weight, early_twin))
    pair = advance(arrived, shards)
    forward = lax.ppermute(forward, "seq", around(1))
    backward = lax.ppermute(backward, "seq", around(-1))
    forward, backward, pair, *state = barrier((forward, backward, pair, *state))
    state = tuple(state)
    final = (
        lax.ppermute(forward[:length], "seq", around(1)),
        lax.ppermute(backward[length:], "seq", around(-1)),
    )
    if packed:
        middle = collect(spread(forward, backward), depth // 2)
        middle_twin = lax.ppermute(middle, "scan", twins)
        q_all, kv_all, middle_twin = barrier((*state, middle_twin))
        state = (q_all, kv_all)
    near_shards = (chips - 3, chips - 2)
    near = advance(spread(forward, backward), near_shards)
    pair, near, *final = barrier((pair, near, *final))
    send(pair, shards)
    send(near, near_shards)
    held, others = others, []
    last = [(array, 0) for array in final]
    send(advance(last, (chips - 1,)), (chips - 1,))
    others = held + others
    if packed:
        late = collect(last, depth // 2)
        late_twin = lax.ppermute(late, "scan", twins)
    q_all, kv_all = state
    attended = attend(
        key_blocks,
        key_counts,
        q_all,
        kv_all,
        [other for other, _ in others],
        chips,
        group,
        heads,
        tuple(range(chips)),
        tuple(held for _, held in others),
    )[1:]
    if packed:
        first, middle_twin, late_twin = barrier((attended[0], middle_twin, late_twin))
        attended = [first, *attended[1:]]
        own_half = pair_rows(
            [(early, early_twin), (middle, middle_twin), (late, late_twin)], chips, True
        )
        other_half = lax.ppermute(own_half, "seq", swap)
        out_weights = [half.reshape(D // 2, D) for half in (own_half, other_half)]
    got = [attended[0]] + [lax.ppermute(attended[k], "seq", across(k)) for k in range(1, chips)]

    share = PROBES // ranks
    split = share % 16 == 0
    layer_out, *parts = tail(
        got,
        out_weights,
        tokens,
        probe_gain.reshape(1, D),
        probe_queries,
        chips,
        group,
        heads,
        split,
    )
    if split:
        mine, theirs = parts
        blocks = deal(mine, lax.ppermute(theirs, "seq", swap), chips)
        joined = [blocks[0]] + [
            lax.ppermute(blocks[k], "seq", across(k)) for k in range(1, chips)
        ]
        return layer_out, join(joined)
    rows = lax.all_to_all(
        parts[0].reshape(ranks, share, D + STATS), "seq", split_axis=0, concat_axis=0, tiled=True
    ).astype(F32)
    logs = rows[:, :, D : D + 3 * HEADS].reshape(ranks, share, 3, HEADS).sum(axis=2)
    factors = jnp.exp(logs - jnp.max(logs, axis=0, keepdims=True))
    factors = factors / jnp.sum(factors, axis=0, keepdims=True)
    probe_out = jnp.sum(jnp.repeat(factors, HEAD_DIM, axis=2) * rows[:, :, :D], axis=0)
    return layer_out, probe_out


def solution(mesh):
    return jax.shard_map(
        per_device,
        mesh=mesh,
        in_specs=(
            P(("scan", "seq"), None),
            P(),
            P("seq", None),
            P("seq", None),
            P("seq", None),
            P("seq", None),
            P(),
            P(),
            P("scan", None),
            P("scan"),
        ),
        out_specs=(P(("scan", "seq"), None), P(("scan", "seq"), None)),
        check_vma=False,
    )
```

```python
import functools
import math

import jax
import jax.numpy as jnp
from jax import lax
from jax.experimental import pallas as pl
from jax.experimental.pallas import tpu as pltpu
from jax.sharding import PartitionSpec as P

D = 1024
HEADS = 16
HEAD_DIM = 64
PROBES = 256
BLOCK = 128
MAXK = 8
TOK_DEV = 256
STATS = 128
CHUNK = 4
EPS = 1e-05
SCALE = 1.0 / math.sqrt(HEAD_DIM)
EXP2_SCALE = SCALE / math.log(2.0)
BF16 = jnp.bfloat16
F32 = jnp.float32
NT = (((1,), (1,)), ((), ()))
VMEM_BYTES = 28 * 1024 * 1024


def whole():
    return pl.BlockSpec(memory_space=pltpu.VMEM)


def scalars():
    return pl.BlockSpec(memory_space=pltpu.SMEM)


def params():
    return pltpu.CompilerParams(vmem_limit_bytes=VMEM_BYTES)


def layer_norm(values, gain):
    wide = values.astype(F32)
    center = wide - jnp.mean(wide, axis=-1, keepdims=True)
    spread = jnp.mean(center * center, axis=-1, keepdims=True)
    return (center * lax.rsqrt(spread + EPS) * gain).astype(BF16)


def head_masked(block, heads):
    if heads == 1:
        return block
    lanes = lax.broadcasted_iota(jnp.int32, block.shape, 1) // HEAD_DIM
    zero = jnp.zeros_like(block)
    return jnp.concatenate([jnp.where(lanes == h, block, zero) for h in range(heads)], axis=0)


def chip_and_core():
    rank = lax.axis_index("seq")
    return lax.shift_right_logical(rank, 1), lax.bitwise_and(rank, 1)


def twin():
    return lax.bitwise_and(lax.axis_index("scan"), 1)


def ring_owners(chip, chips):
    half = lax.shift_right_logical(chip, 1)
    position = jnp.where(lax.bitwise_and(chip, 1) == 1, chips - 1 - half, half)
    offsets = [0]
    for s in range(1, chips // 2):
        offsets += [-s, s]
    offsets.append(chips // 2)
    owners = []
    for offset in offsets:
        spot = lax.rem(position + (offset + chips), chips)
        owners.append(jnp.where(spot < chips // 2, 2 * spot, 2 * (chips - 1 - spot) + 1))
    return owners


def prepare_kernel(
    width, tokens_ref, query_ref, key_ref, value_ref, out_ref, load_ref, mine_ref, theirs_ref, rows_ref, sems
):
    chip, core = chip_and_core()
    rows = out_ref.shape[0] // 4
    half = TOK_DEV // 2
    step = half + rows
    copies = []
    for part in range(2):
        start = pl.multiple_of(twin() * (2 * rows) + part * rows, rows)
        to = load_ref.at[part * step : part * step + half, :]
        copies.append((tokens_ref.at[part * half : (part + 1) * half, :], to))
        to = load_ref.at[part * step + half : (part + 1) * step, :]
        copies.append((out_ref.at[pl.ds(start, rows), :], to))
    for i, ref in enumerate((query_ref, key_ref, value_ref)):
        copies.append((ref, rows_ref.at[i]))
    copies = [pltpu.make_async_copy(a, b, sems.at[i]) for i, (a, b) in enumerate(copies)]
    for copy in copies:
        copy.start()
    for copy in copies:
        copy.wait()
    for ref, side in ((mine_ref, core), (theirs_ref, 1 - core)):
        for j in range(2):
            target = lax.bitwise_xor(chip, 2 * twin() + side + 4 * j)
            lanes = pl.ds(pl.multiple_of(target * width, width), width)
            for i in range(3):
                ref[j, :, i * width : (i + 1) * width] = rows_ref[i, :, lanes]


def prepare(tokens, weights, out_weight, width):
    rows = out_weight.shape[0] // 2
    block = jax.ShapeDtypeStruct((2, 2 * rows, 3 * width), BF16)
    return pl.pallas_call(
        functools.partial(prepare_kernel, width),
        out_shape=(jax.ShapeDtypeStruct((TOK_DEV + rows, D), BF16), block, block),
        in_specs=[pl.BlockSpec(memory_space=pltpu.HBM)] * 5,
        out_specs=(whole(),) * 3,
        scratch_shapes=[pltpu.VMEM((3, 2 * rows, D), BF16), pltpu.SemaphoreType.DMA((7,))],
        compiler_params=params(),
        name="prepare",
    )(*(pltpu.with_memory_space_constraint(x, pltpu.HBM) for x in (tokens, *weights, out_weight)))


def bundle_kernel(mine_ref, got_ref, *outs):
    _, core = chip_and_core()
    rows = mine_ref.shape[1]
    for j, ref in enumerate(outs):
        mine, got = mine_ref[j], got_ref[j]
        ref[:rows, :] = jnp.where(core == 0, mine, got)
        ref[rows:, :] = jnp.where(core == 0, got, mine)


def bundle(mine, got):
    _, rows, columns = mine.shape
    return pl.pallas_call(
        bundle_kernel,
        out_shape=[jax.ShapeDtypeStruct((2 * rows, columns), BF16)] * 2,
        in_specs=[whole()] * 2,
        out_specs=[whole()] * 2,
        compiler_params=params(),
        name="bundle",
    )(mine, got)


def keep_kernel(own_ref, near_ref, far_ref, out_ref):
    _, core = chip_and_core()
    out_ref[0] = jnp.where(2 * twin() + core == 0, own_ref[...], near_ref[...])
    out_ref[1] = far_ref[...]


def keep(own, near, far):
    return pl.pallas_call(
        keep_kernel,
        out_shape=jax.ShapeDtypeStruct((2,) + own.shape, BF16),
        in_specs=[whole()] * 3,
        out_specs=whole(),
        compiler_params=params(),
        name="keep",
    )(own, near, far)


def assemble_kernel(own_ref, twin_ref, other_ref, out_ref, stage):
    chip, core = chip_and_core()
    role = 2 * twin() + core
    for j in range(2):
        for flip, block in (
            (0, own_ref[j]),
            (2, twin_ref[j]),
            (1, other_ref[j]),
            (3, other_ref[2 + j]),
        ):
            source = lax.bitwise_xor(chip, lax.bitwise_xor(role, flip) + 4 * j)
            stage[source] = block
    out_ref[...] = stage[...].reshape(out_ref.shape)


def assemble(own, twin_blocks, other):
    _, rows, columns = own.shape
    return pl.pallas_call(
        assemble_kernel,
        out_shape=jax.ShapeDtypeStruct((8 * rows, columns), BF16),
        in_specs=[whole()] * 3,
        out_specs=whole(),
        scratch_shapes=[pltpu.VMEM((8, rows, columns), BF16)],
        compiler_params=params(),
        name="assemble",
    )(own, twin_blocks, other)


def gather_blocks_kernel(picks, ordered, *refs):
    chip, _ = chip_and_core()
    for at, (i, j) in enumerate(picks):
        refs[-1][lax.bitwise_xor(chip, at) if ordered else at] = refs[i][j]


def gather_blocks(blocks, ordered):
    arrays, picks = [], []
    for array, j in blocks:
        if not any(array is one for one in arrays):
            arrays.append(array)
        picks.append(([array is one for one in arrays].index(True), j))
    return pl.pallas_call(
        functools.partial(gather_blocks_kernel, tuple(picks), ordered),
        out_shape=jax.ShapeDtypeStruct((len(blocks),) + arrays[0].shape[1:], BF16),
        in_specs=[whole()] * len(arrays),
        out_specs=whole(),
        compiler_params=params(),
        name="gather_blocks",
    )(*arrays)


def collect_kernel(places, *refs):
    out_ref = refs[-1]
    rows = out_ref.shape[1] // 2
    for i, at in enumerate(places):
        part = i % 2
        out_ref[i // 2, part * rows : (part + 1) * rows, :] = refs[i][at : at + rows, :]


def collect(pieces, rows):
    places = tuple(at + TOK_DEV // 2 for _, at in pieces)
    return pl.pallas_call(
        functools.partial(collect_kernel, places),
        out_shape=jax.ShapeDtypeStruct((len(pieces) // 2, rows, D), BF16),
        in_specs=[whole()] * len(pieces),
        out_specs=whole(),
        compiler_params=params(),
        name="collect",
    )(*(array for array, _ in pieces))


def pair_rows_kernel(chips, ringed, *refs):
    out_ref = refs[-1]
    mine = twin()
    chip, _ = chip_and_core()
    owners = ring_owners(chip, chips) if ringed else range(chips)
    at = 0
    for own_ref, twin_ref in zip(refs[0:-1:2], refs[1:-1:2]):
        for i in range(own_ref.shape[0]):
            out_ref[owners[at], mine] = own_ref[i]
            out_ref[owners[at], 1 - mine] = twin_ref[i]
            at += 1


def pair_rows(pairs, chips, ringed):
    rows, columns = pairs[0][0].shape[1:]
    flat = [p for pair in pairs for p in pair]
    return pl.pallas_call(
        functools.partial(pair_rows_kernel, chips, ringed),
        out_shape=jax.ShapeDtypeStruct((chips, 2, rows, columns), BF16),
        in_specs=[whole()] * len(flat),
        out_specs=whole(),
        compiler_params=params(),
        name="pair_rows",
    )(*flat)


def weave_kernel(own_ref, other_ref, out_ref):
    _, core = chip_and_core()
    chips, rows, columns = own_ref.shape
    for c in range(chips):
        own, other = own_ref[c], other_ref[c]
        out_ref[2 * c * rows : (2 * c + 1) * rows, :] = jnp.where(core == 0, own, other)
        out_ref[(2 * c + 1) * rows : (2 * c + 2) * rows, :] = jnp.where(core == 0, other, own)


def weave(own, other):
    chips, two, rows, columns = own.shape
    own, other = (x.reshape(chips, two * rows, columns) for x in (own, other))
    return pl.pallas_call(
        weave_kernel,
        out_shape=jax.ShapeDtypeStruct((4 * chips * rows, columns), BF16),
        in_specs=[whole()] * 2,
        out_specs=whole(),
        compiler_params=params(),
        name="weave",
    )(own, other)


def shard_blocks(owner, core):
    first = (owner * 2 + core) * (TOK_DEV // BLOCK)
    return [first + u for u in range(TOK_DEV // BLOCK)]


def absorb(pair_ref, kv_all, owners, core):
    blocks = TOK_DEV // BLOCK
    for t, owner in enumerate(owners):
        for u, block in enumerate(shard_blocks(owner, core)):
            kv_all[block] = pair_ref[t * blocks + u]


def project_kernel(chips, starts, width, shards, before, *refs):
    n = len(starts)
    inputs, (gain_ref, weight_ref), (q_all, kv_all, pair_ref) = refs[:n], refs[n : n + 2], refs[-3:]
    chip, core = chip_and_core()
    owners = ring_owners(chip, chips)
    places = [(ref, at) for ref, spots in zip(inputs, starts) for at in spots]
    for begin in range(0, len(places), CHUNK):
        segments = [ref[at : at + BLOCK, :] for ref, at in places[begin : begin + CHUNK]]
        normed = layer_norm(jnp.concatenate(segments, axis=0), gain_ref[...])
        result = jnp.dot(normed, weight_ref[...], preferred_element_type=F32)
        for j in range(len(segments)):
            i = begin + j
            rows = result[j * BLOCK : (j + 1) * BLOCK]
            t, u = divmod(i, TOK_DEV // BLOCK)
            q_all[owners[shards[t]] * (TOK_DEV // BLOCK) + u] = rows[:, :width].astype(BF16)
            pair_ref[i, 0, :, :width] = rows[:, width : 2 * width].astype(BF16)
            pair_ref[i, 1, :width, :] = jnp.transpose(rows[:, 2 * width :]).astype(BF16)
            if width < BLOCK:
                pair_ref[i, 0, :, width:] = jnp.zeros((BLOCK, BLOCK - width), BF16)
                pair_ref[i, 1, width:, :] = jnp.zeros((BLOCK - width, BLOCK), BF16)
    absorb(pair_ref, kv_all, [owners[s] for s in shards], core)
    for i, held in enumerate(before):
        absorb(refs[n + 4 + i], kv_all, [owners[s] for s in held], 1 - core)


def project(pieces, starts, gain, weight, width, chips, shards, before, state):
    blocks = sum(len(s) for s in starts)
    n = len(pieces)
    total = chips * (TOK_DEV // BLOCK)
    return pl.pallas_call(
        functools.partial(project_kernel, chips, starts, width, shards, before),
        out_shape=(
            jax.ShapeDtypeStruct((total, BLOCK, width), BF16),
            jax.ShapeDtypeStruct((2 * total, 2, BLOCK, BLOCK), BF16),
            jax.ShapeDtypeStruct((blocks, 2, BLOCK, BLOCK), BF16),
        ),
        in_specs=[whole()] * (n + 2 + len(state)),
        out_specs=(whole(),) * 3,
        input_output_aliases={n + 2: 0, n + 3: 1} if state else {},
        compiler_params=params(),
        name="project",
    )(*pieces, gain, weight, *state)


def attend_kernel(chips, group, heads, steps, last, lists_ref, counts_ref, q_all, *refs):
    width = heads * HEAD_DIM
    outs, mixed = refs[-1 - len(steps) : -1], refs[-1]
    chip, core = chip_and_core()
    kv_all = refs[0]
    if last:
        kv_all = refs[1 + len(last)]
        owners = ring_owners(chip, chips)
        for i, held in enumerate(last):
            absorb(refs[1 + i], kv_all, [owners[s] for s in held], 1 - core)
    member = lax.rem(chip, group)
    blocks = TOK_DEV // BLOCK
    per_piece = blocks // group

    def place_of(index):
        target = lax.bitwise_xor(chip, steps[0] + lax.div(index, per_piece))
        within = member * per_piece + lax.rem(index, per_piece)
        return target * blocks + within, (target * 2 + core) * blocks + within

    def attend_block(index, used):
        row, block = place_of(index)
        count = counts_ref[block]
        picked = [lists_ref[block, s] for s in range(used)]
        stacked = head_masked(q_all[row], heads)
        scores = []
        for s, p in enumerate(picked):
            one = lax.dot_general(
                kv_all[p, 0][:, :width], stacked, NT, preferred_element_type=F32
            )
            if s:
                one = one + jnp.where(s < count, 0.0, -jnp.inf).astype(F32)
            scores.append(one)
        scores = jnp.concatenate(scores, axis=0)
        top = jnp.max(scores, axis=0, keepdims=True)
        weights = jnp.exp2((scores - top) * EXP2_SCALE)
        total = jnp.sum(weights, axis=0, keepdims=True)
        values = jnp.concatenate([kv_all[p, 1] for p in picked], axis=1)[:width]
        full = jnp.dot(values, weights.astype(BF16), preferred_element_type=F32)
        full = full * (1.0 / total)
        result = jnp.concatenate(
            [
                full[h * HEAD_DIM : (h + 1) * HEAD_DIM, h * BLOCK : (h + 1) * BLOCK]
                for h in range(heads)
            ],
            axis=0,
        )
        return jnp.transpose(result).astype(BF16)

    def one_pair(pair, carry):
        first, second = 2 * pair, 2 * pair + 1
        most = jnp.maximum(counts_ref[place_of(first)[1]], counts_ref[place_of(second)[1]])
        for used in range(1, MAXK + 1):

            @pl.when(most == used)
            def _(used=used):
                one, two = attend_block(first, used), attend_block(second, used)
                mixed[first] = one
                mixed[second] = two

        return carry

    lax.fori_loop(0, len(steps) * per_piece // 2, one_pair, 0)
    for k in range(len(steps)):
        for part in range(per_piece):
            outs[k][part * BLOCK : (part + 1) * BLOCK, :] = mixed[k * per_piece + part]


def attend(lists, counts, q_all, kv_all, extra, chips, group, heads, steps, last):
    width = heads * HEAD_DIM
    piece = TOK_DEV // group
    kv_shape = [jax.ShapeDtypeStruct(kv_all.shape, BF16)] if last else []
    return pl.pallas_call(
        functools.partial(attend_kernel, chips, group, heads, steps, last),
        out_shape=kv_shape + [jax.ShapeDtypeStruct((piece, width), BF16)] * len(steps),
        in_specs=[scalars()] * 2 + [whole()] * (2 + len(extra)),
        out_specs=[whole()] * (len(kv_shape) + len(steps)),
        input_output_aliases={3: 0} if last else {},
        scratch_shapes=[pltpu.VMEM((len(steps) * (piece // BLOCK), BLOCK, width), BF16)],
        compiler_params=params(),
        name="attend",
    )(lists, counts, q_all, kv_all, *extra)


def tail_kernel(chips, group, heads, split, parts, *refs):
    width = heads * HEAD_DIM
    sets = HEADS // heads
    piece = TOK_DEV // group
    got = refs[:chips]
    tokens_ref, gain_ref, probe_ref, *weight_refs = refs[chips : chips + 3 + parts]
    layer_ref, *part_refs, stage = refs[chips + 3 + parts :]
    chip, core = chip_and_core()
    for k in range(chips):
        source = lax.bitwise_xor(chip, k)
        if group == 1:
            stage[source] = got[k][...]
        else:
            stage[source // group, pl.ds(pl.multiple_of(source % group * piece, piece), piece), :] = got[k][...]
    if parts == 1:
        attended = jnp.concatenate([stage[s] for s in range(sets)], axis=1)
        projected = jnp.dot(attended, weight_refs[0][...], preferred_element_type=F32)
    else:
        left = lax.broadcasted_iota(jnp.int32, (TOK_DEV, width), 1) < HEAD_DIM
        ours, theirs = [], []
        for s in range(0, sets, 2):
            one, two = stage[s], stage[s + 1]
            first = jnp.where(left, one, pltpu.roll(two, HEAD_DIM, axis=1))
            second = jnp.where(left, pltpu.roll(one, HEAD_DIM, axis=1), two)
            ours.append(jnp.where(core == 0, first, second))
            theirs.append(jnp.where(core == 0, second, first))
        projected = jnp.dot(
            jnp.concatenate(ours, axis=1), weight_refs[0][...], preferred_element_type=F32
        )
        projected += jnp.dot(
            jnp.concatenate(theirs, axis=1), weight_refs[1][...], preferred_element_type=F32
        )
    layer = (tokens_ref[...].astype(F32) + projected).astype(BF16)
    layer_ref[...] = layer
    pooled = layer_norm(layer, gain_ref[...])
    rows = []

    def emit(lo, value):
        hi = lo + value.shape[1]
        if not split:
            part_refs[0][:, lo:hi] = value.astype(BF16)
            return
        lines, share = chips // 2, PROBES // (2 * chips)
        shaped = value.reshape(lines, 2, 2, share, value.shape[1])
        side = lax.bitwise_and(chip, 1)
        near = jnp.where(side == 0, shaped[:, 0], shaped[:, 1])
        far = jnp.where(side == 0, shaped[:, 1], shaped[:, 0])
        for i, rows_of in enumerate((near, far)):
            mine = jnp.where(core == 0, rows_of[:, 0], rows_of[:, 1])
            theirs = jnp.where(core == 0, rows_of[:, 1], rows_of[:, 0])
            part_refs[2 * i][:, lo:hi] = mine.reshape(lines * share, -1).astype(BF16)
            part_refs[2 * i + 1][:, lo:hi] = theirs.reshape(lines * share, -1).astype(BF16)

    for pair in range(HEADS // 2):
        lo = pair * 2 * HEAD_DIM
        own = pooled[:, lo : lo + 2 * HEAD_DIM]
        stacked = head_masked(probe_ref[:, lo : lo + 2 * HEAD_DIM], 2)
        scores = lax.dot_general(own, stacked, NT, preferred_element_type=F32)
        top = jnp.max(scores, axis=0, keepdims=True)
        weights = jnp.exp2((scores - top) * EXP2_SCALE)
        total = jnp.sum(weights, axis=0, keepdims=True)
        flipped = jnp.transpose(own.astype(F32)).astype(BF16)
        full = jnp.dot(flipped, weights.astype(BF16), preferred_element_type=F32) / total
        result = jnp.concatenate([full[:HEAD_DIM, :PROBES], full[HEAD_DIM:, PROBES:]], axis=0)
        emit(lo, jnp.transpose(result))
        logs = top * SCALE + jnp.log(total)
        rows += [logs[:, :PROBES], logs[:, PROBES:]]
    logs = jnp.concatenate(rows, axis=0)
    high = logs.astype(BF16).astype(F32)
    middle = (logs - high).astype(BF16).astype(F32)
    low = logs - high - middle
    rest = jnp.zeros((STATS - 3 * HEADS, PROBES), F32)
    emit(D, jnp.transpose(jnp.concatenate([high, middle, low, rest], axis=0)))


def tail(got, weights, tokens, gain, probes, chips, group, heads, split):
    width = heads * HEAD_DIM
    rows = PROBES // 4 if split else PROBES
    return pl.pallas_call(
        functools.partial(tail_kernel, chips, group, heads, split, len(weights)),
        out_shape=[jax.ShapeDtypeStruct((TOK_DEV, D), BF16)]
        + [jax.ShapeDtypeStruct((rows, D + STATS), BF16)] * (4 if split else 1),
        in_specs=[whole()] * (chips + 3 + len(weights)),
        out_specs=[whole()] * (5 if split else 2),
        scratch_shapes=[pltpu.VMEM((HEADS // heads, TOK_DEV, width), BF16)],
        compiler_params=params(),
        name="tail",
    )(*got, tokens, gain, probes, *weights)


def read_logs(block):
    pick = lax.broadcasted_iota(jnp.int32, (STATS, STATS), 0)
    head = lax.broadcasted_iota(jnp.int32, (STATS, STATS), 1)
    gather = ((pick < 3 * HEADS) & (pick % HEADS == head)).astype(BF16)
    return jnp.dot(block, gather, preferred_element_type=F32)


def spread_heads(factors):
    row = lax.broadcasted_iota(jnp.int32, (STATS, D), 0)
    lane = lax.broadcasted_iota(jnp.int32, (STATS, D), 1)
    widen = (lane // HEAD_DIM == row).astype(F32)
    return jnp.dot(factors, widen, preferred_element_type=F32, precision=lax.Precision.HIGHEST)


def blend(blocks):
    logs = [read_logs(b[:, D:]) for b in blocks]
    top = functools.reduce(jnp.maximum, logs)
    shares = [jnp.exp(one - top) for one in logs]
    total = functools.reduce(jnp.add, shares)
    rows = blocks[0].shape[0]
    wide = spread_heads(jnp.concatenate([s / total for s in shares], axis=0))
    value = 0.0
    for i, b in enumerate(blocks):
        value = value + wide[i * rows : (i + 1) * rows] * b[:, :D].astype(F32)
    return value, top + jnp.log(total)


def repack(value, logs):
    high = logs.astype(BF16).astype(F32)
    middle = (logs - high).astype(BF16).astype(F32)
    low = logs - high - middle
    rest = jnp.zeros((value.shape[0], STATS - 3 * HEADS), F32)
    return jnp.concatenate(
        [value, high[:, :HEADS], middle[:, :HEADS], low[:, :HEADS], rest], axis=1
    ).astype(BF16)


def deal_kernel(count, *refs):
    outs, stage = refs[count:-1], refs[-1]
    chip, _ = chip_and_core()
    line = lax.shift_right_logical(chip, 1)
    packed = repack(*blend([ref[...] for ref in refs[:count]]))
    stage[...] = packed.reshape(stage.shape)
    for k in range(len(outs)):
        outs[k][...] = stage[lax.bitwise_xor(line, k)]


def deal(blocks, parts):
    share = blocks[0].shape[0] // parts
    return pl.pallas_call(
        functools.partial(deal_kernel, len(blocks)),
        out_shape=[jax.ShapeDtypeStruct((share, D + STATS), BF16)] * parts,
        in_specs=[whole()] * len(blocks),
        out_specs=[whole()] * parts,
        scratch_shapes=[pltpu.VMEM((parts, share, D + STATS), BF16)],
        compiler_params=params(),
        name="deal",
    )(*blocks)


def last_kernel(*refs):
    refs[-1][...] = blend([r[...] for r in refs[:-1]])[0]


def join(parts):
    return pl.pallas_call(
        last_kernel,
        out_shape=jax.ShapeDtypeStruct((parts[0].shape[0], D), F32),
        in_specs=[whole()] * len(parts),
        out_specs=whole(),
        compiler_params=params(),
        name="join",
    )(*parts)


def per_device(
    tokens,
    ln_gain,
    w_query,
    w_key,
    w_value,
    w_out,
    probe_gain,
    probe_queries,
    key_blocks,
    key_counts,
):
    ranks = lax.axis_size("seq")
    chips = ranks // 2
    heads = max(1, HEADS // chips)
    group = max(1, chips // HEADS)
    sets = HEADS // heads
    width = heads * HEAD_DIM
    myself = lax.axis_index("seq")
    core = myself % 2
    order = list(range(0, chips, 2)) + list(range(chips - 1, 0, -2))
    swap = [(i, i ^ 1) for i in range(ranks)]
    same_core = [[2 * c + k for c in range(chips)] for k in range(2)]

    def around(shift):
        return [
            (order[i] * 2 + k, order[(i + shift) % chips] * 2 + k)
            for i in range(chips)
            for k in range(2)
        ]

    def across(k):
        return [(2 * c + q, 2 * (c ^ k) + q) for c in range(chips) for q in range(2)]

    twins = [(i, i ^ 1) for i in range(lax.axis_size("scan"))]
    barrier = lax.optimization_barrier
    depth = w_query.shape[0]
    gain = ln_gain.reshape(1, D)
    half = TOK_DEV // 2
    packed = depth == 64 and chips == 8

    if packed:
        load, mine, theirs = prepare(tokens, (w_query, w_key, w_value), w_out, width)
        sent = bundle(mine, lax.ppermute(theirs, "seq", swap))

        def serve(offset):
            pairs = []
            for x in range(lax.axis_size("scan")):
                for rank in range(ranks):
                    flip = 2 * (x & 1) + (rank & 1) + offset
                    if flip:
                        pairs.append((x * ranks + rank, x * ranks + (rank ^ (2 * flip))))
            return pairs

        moved = [lax.ppermute(sent[j], ("scan", "seq"), serve(4 * j)) for j in range(2)]
    else:
        columns = jnp.stack([w_query, w_key, w_value]).reshape(3, depth, sets, width)
        columns = jnp.transpose(columns, (2, 1, 0, 3)).reshape(sets, depth, 3 * width)
        columns = jnp.repeat(columns, group, axis=0)
        here = lax.all_to_all(
            columns, "seq", split_axis=0, concat_axis=0, tiled=True, axis_index_groups=same_core
        )
        there = lax.ppermute(here, "seq", swap)
        even = jnp.where(core == 0, here, there)
        odd = jnp.where(core == 0, there, here)
        weight = jnp.stack([even, odd], axis=1).reshape(D, 3 * width)
        out_weights = [lax.all_gather(w_out, "seq", axis=0, tiled=True)]

    load = load if packed else tokens
    length = load.shape[0] // 2
    forward = backward = load

    def spread(*shards):
        return [(shard, at) for shard in shards for at in (0, length)]

    state, others = (), []

    def advance(pieces, shards):
        nonlocal state, others
        q_all, kv_all, pair = project(
            [array for array, _ in pieces],
            tuple((at,) for _, at in pieces),
            gain,
            weight,
            width,
            chips,
            shards,
            tuple(held for _, held in others),
            state + tuple(other for other, _ in others),
        )
        state, others = (q_all, kv_all), []
        return pair

    def send(pair, shards):
        others.append((lax.ppermute(pair, "seq", swap), shards))

    arrived, shards = spread(load), (0,)
    for s in range(1, chips // 2 - 1):
        forward = lax.ppermute(forward, "seq", around(1))
        backward = lax.ppermute(backward, "seq", around(-1))
        if packed and s == 1:
            forward, backward, *moved = barrier((forward, backward, *moved))
        if packed and s == 2:
            blocks = keep(sent[0], *moved)
            twin_blocks = lax.ppermute(blocks, "scan", twins)
            joint = gather_blocks(
                [(blocks, 0), (blocks, 1), (twin_blocks, 0), (twin_blocks, 1)], False
            )
            weight = assemble(blocks, twin_blocks, lax.ppermute(joint, "seq", swap))
            forward, backward, weight = barrier((forward, backward, weight))
        arrived += spread(forward, backward)
        shards += (2 * s - 1, 2 * s)
    if packed:
        early = collect(arrived, depth // 2)
        early_twin = lax.ppermute(early, "scan", twins)
        weight, early_twin = barrier((weight, early_twin))
    pair = advance(arrived, shards)
    forward = lax.ppermute(forward, "seq", around(1))
    backward = lax.ppermute(backward, "seq", around(-1))
    forward, backward, pair, *state = barrier((forward, backward, pair, *state))
    state = tuple(state)
    final = (
        lax.ppermute(forward[:length], "seq", around(1)),
        lax.ppermute(backward[length:], "seq", around(-1)),
    )
    if packed:
        middle = collect(spread(forward, backward), depth // 2)
        middle_twin = lax.ppermute(middle, "scan", twins)
        q_all, kv_all, middle_twin = barrier((*state, middle_twin))
        state = (q_all, kv_all)
    near_shards = (chips - 3, chips - 2)
    near = advance(spread(forward, backward), near_shards)
    pair, near, *final = barrier((pair, near, *final))
    send(pair, shards)
    send(near, near_shards)
    held, others = others, []
    last = [(array, 0) for array in final]
    send(advance(last, (chips - 1,)), (chips - 1,))
    others = held + others
    if packed:
        late = collect(last, depth // 2)
        late_twin = lax.ppermute(late, "scan", twins)
    q_all, kv_all = state
    attended = attend(
        key_blocks,
        key_counts,
        q_all,
        kv_all,
        [other for other, _ in others],
        chips,
        group,
        heads,
        tuple(range(chips)),
        tuple(held for _, held in others),
    )[1:]
    if packed:
        first, middle_twin, late_twin = barrier((attended[0], middle_twin, late_twin))
        attended = [first, *attended[1:]]
        own_half = pair_rows(
            [(early, early_twin), (middle, middle_twin), (late, late_twin)], chips, True
        )
        other_half = lax.ppermute(own_half, "seq", swap)
        out_weights = [half.reshape(D // 2, D) for half in (own_half, other_half)]
    got = [attended[0]] + [lax.ppermute(attended[k], "seq", across(k)) for k in range(1, chips)]

    share = PROBES // ranks
    split = share % 16 == 0
    layer_out, *parts = tail(
        got,
        out_weights,
        tokens,
        probe_gain.reshape(1, D),
        probe_queries,
        chips,
        group,
        heads,
        split,
    )
    if split:
        mine, core_part, side_part, both_part = parts
        blocks = [
            mine,
            lax.ppermute(side_part, "seq", across(1)),
            lax.ppermute(both_part, "seq", [(i, i ^ 3) for i in range(ranks)]),
            lax.ppermute(core_part, "seq", swap),
        ]
        lines = deal(blocks, chips // 2)
        joined = [lines[0]] + [
            lax.ppermute(lines[k], "seq", across(2 * k)) for k in range(1, chips // 2)
        ]
        return layer_out, join(joined)
    rows = lax.all_to_all(
        parts[0].reshape(ranks, share, D + STATS), "seq", split_axis=0, concat_axis=0, tiled=True
    ).astype(F32)
    logs = rows[:, :, D : D + 3 * HEADS].reshape(ranks, share, 3, HEADS).sum(axis=2)
    factors = jnp.exp(logs - jnp.max(logs, axis=0, keepdims=True))
    factors = factors / jnp.sum(factors, axis=0, keepdims=True)
    probe_out = jnp.sum(jnp.repeat(factors, HEAD_DIM, axis=2) * rows[:, :, :D], axis=0)
    return layer_out, probe_out


def solution(mesh):
    return jax.shard_map(
        per_device,
        mesh=mesh,
        in_specs=(
            P(("scan", "seq"), None),
            P(),
            P("seq", None),
            P("seq", None),
            P("seq", None),
            P("seq", None),
            P(),
            P(),
            P("scan", None),
            P("scan"),
        ),
        out_specs=(P(("scan", "seq"), None), P(("scan", "seq"), None)),
        check_vma=False,
    )
```

```python
import functools
import math

import jax
import jax.numpy as jnp
from jax import lax
from jax.experimental import pallas as pl
from jax.experimental.pallas import tpu as pltpu
from jax.sharding import PartitionSpec as P

D = 1024
HEADS = 16
HEAD_DIM = 64
PROBES = 256
BLOCK = 128
MAXK = 8
TOK_DEV = 256
STATS = 128
CHUNK = 4
EPS = 1e-05
SCALE = 1.0 / math.sqrt(HEAD_DIM)
EXP2_SCALE = SCALE / math.log(2.0)
BF16 = jnp.bfloat16
F32 = jnp.float32
NT = (((1,), (1,)), ((), ()))
VMEM_BYTES = 28 * 1024 * 1024


def whole():
    return pl.BlockSpec(memory_space=pltpu.VMEM)


def scalars():
    return pl.BlockSpec(memory_space=pltpu.SMEM)


def params():
    return pltpu.CompilerParams(vmem_limit_bytes=VMEM_BYTES)


def layer_norm(values, gain):
    wide = values.astype(F32)
    center = wide - jnp.mean(wide, axis=-1, keepdims=True)
    spread = jnp.mean(center * center, axis=-1, keepdims=True)
    return (center * lax.rsqrt(spread + EPS) * gain).astype(BF16)


def head_masked(block, heads):
    if heads == 1:
        return block
    lanes = lax.broadcasted_iota(jnp.int32, block.shape, 1) // HEAD_DIM
    zero = jnp.zeros_like(block)
    return jnp.concatenate([jnp.where(lanes == h, block, zero) for h in range(heads)], axis=0)


def chip_and_core():
    rank = lax.axis_index("seq")
    return lax.shift_right_logical(rank, 1), lax.bitwise_and(rank, 1)


def twin():
    return lax.bitwise_and(lax.axis_index("scan"), 1)


def ring_owners(chip, chips):
    half = lax.shift_right_logical(chip, 1)
    position = jnp.where(lax.bitwise_and(chip, 1) == 1, chips - 1 - half, half)
    offsets = [0]
    for s in range(1, chips // 2):
        offsets += [-s, s]
    offsets.append(chips // 2)
    owners = []
    for offset in offsets:
        spot = lax.rem(position + (offset + chips), chips)
        owners.append(jnp.where(spot < chips // 2, 2 * spot, 2 * (chips - 1 - spot) + 1))
    return owners


def prepare_kernel(
    width, tokens_ref, query_ref, key_ref, value_ref, out_ref, load_ref, mine_ref, theirs_ref, rows_ref, sems
):
    chip, core = chip_and_core()
    rows = out_ref.shape[0] // 4
    half = TOK_DEV // 2
    step = half + rows
    copies = []
    for part in range(2):
        start = pl.multiple_of(twin() * (2 * rows) + part * rows, rows)
        to = load_ref.at[part * step : part * step + half, :]
        copies.append((tokens_ref.at[part * half : (part + 1) * half, :], to))
        to = load_ref.at[part * step + half : (part + 1) * step, :]
        copies.append((out_ref.at[pl.ds(start, rows), :], to))
    for i, ref in enumerate((query_ref, key_ref, value_ref)):
        copies.append((ref, rows_ref.at[i]))
    copies = [pltpu.make_async_copy(a, b, sems.at[i]) for i, (a, b) in enumerate(copies)]
    for copy in copies:
        copy.start()
    for copy in copies:
        copy.wait()
    for ref, side in ((mine_ref, core), (theirs_ref, 1 - core)):
        for j in range(2):
            target = lax.bitwise_xor(chip, 2 * twin() + side + 4 * j)
            lanes = pl.ds(pl.multiple_of(target * width, width), width)
            for i in range(3):
                ref[j, :, i * width : (i + 1) * width] = rows_ref[i, :, lanes]


def prepare(tokens, weights, out_weight, width):
    rows = out_weight.shape[0] // 2
    block = jax.ShapeDtypeStruct((2, 2 * rows, 3 * width), BF16)
    return pl.pallas_call(
        functools.partial(prepare_kernel, width),
        out_shape=(jax.ShapeDtypeStruct((TOK_DEV + rows, D), BF16), block, block),
        in_specs=[pl.BlockSpec(memory_space=pltpu.HBM)] * 5,
        out_specs=(whole(),) * 3,
        scratch_shapes=[pltpu.VMEM((3, 2 * rows, D), BF16), pltpu.SemaphoreType.DMA((7,))],
        compiler_params=params(),
        name="prepare",
    )(*(pltpu.with_memory_space_constraint(x, pltpu.HBM) for x in (tokens, *weights, out_weight)))


def bundle_kernel(mine_ref, got_ref, *outs):
    _, core = chip_and_core()
    rows = mine_ref.shape[1]
    for j, ref in enumerate(outs):
        mine, got = mine_ref[j], got_ref[j]
        ref[:rows, :] = jnp.where(core == 0, mine, got)
        ref[rows:, :] = jnp.where(core == 0, got, mine)


def bundle(mine, got):
    _, rows, columns = mine.shape
    return pl.pallas_call(
        bundle_kernel,
        out_shape=[jax.ShapeDtypeStruct((2 * rows, columns), BF16)] * 2,
        in_specs=[whole()] * 2,
        out_specs=[whole()] * 2,
        compiler_params=params(),
        name="bundle",
    )(mine, got)


def keep_kernel(own_ref, near_ref, far_ref, out_ref):
    _, core = chip_and_core()
    out_ref[0] = jnp.where(2 * twin() + core == 0, own_ref[...], near_ref[...])
    out_ref[1] = far_ref[...]


def keep(own, near, far):
    return pl.pallas_call(
        keep_kernel,
        out_shape=jax.ShapeDtypeStruct((2,) + own.shape, BF16),
        in_specs=[whole()] * 3,
        out_specs=whole(),
        compiler_params=params(),
        name="keep",
    )(own, near, far)


def assemble_kernel(own_ref, twin_ref, other_ref, out_ref, stage):
    chip, core = chip_and_core()
    role = 2 * twin() + core
    for j in range(2):
        for flip, block in (
            (0, own_ref[j]),
            (2, twin_ref[j]),
            (1, other_ref[j]),
            (3, other_ref[2 + j]),
        ):
            source = lax.bitwise_xor(chip, lax.bitwise_xor(role, flip) + 4 * j)
            stage[source] = block
    out_ref[...] = stage[...].reshape(out_ref.shape)


def assemble(own, twin_blocks, other):
    _, rows, columns = own.shape
    return pl.pallas_call(
        assemble_kernel,
        out_shape=jax.ShapeDtypeStruct((8 * rows, columns), BF16),
        in_specs=[whole()] * 3,
        out_specs=whole(),
        scratch_shapes=[pltpu.VMEM((8, rows, columns), BF16)],
        compiler_params=params(),
        name="assemble",
    )(own, twin_blocks, other)


def gather_blocks_kernel(picks, ordered, *refs):
    chip, _ = chip_and_core()
    for at, (i, j) in enumerate(picks):
        refs[-1][lax.bitwise_xor(chip, at) if ordered else at] = refs[i][j]


def gather_blocks(blocks, ordered):
    arrays, picks = [], []
    for array, j in blocks:
        if not any(array is one for one in arrays):
            arrays.append(array)
        picks.append(([array is one for one in arrays].index(True), j))
    return pl.pallas_call(
        functools.partial(gather_blocks_kernel, tuple(picks), ordered),
        out_shape=jax.ShapeDtypeStruct((len(blocks),) + arrays[0].shape[1:], BF16),
        in_specs=[whole()] * len(arrays),
        out_specs=whole(),
        compiler_params=params(),
        name="gather_blocks",
    )(*arrays)


def collect_kernel(places, *refs):
    out_ref = refs[-1]
    rows = out_ref.shape[1] // 2
    for i, at in enumerate(places):
        part = i % 2
        out_ref[i // 2, part * rows : (part + 1) * rows, :] = refs[i][at : at + rows, :]


def collect(pieces, rows):
    places = tuple(at + TOK_DEV // 2 for _, at in pieces)
    return pl.pallas_call(
        functools.partial(collect_kernel, places),
        out_shape=jax.ShapeDtypeStruct((len(pieces) // 2, rows, D), BF16),
        in_specs=[whole()] * len(pieces),
        out_specs=whole(),
        compiler_params=params(),
        name="collect",
    )(*(array for array, _ in pieces))


def pair_rows_kernel(chips, ringed, *refs):
    out_ref = refs[-1]
    mine = twin()
    chip, _ = chip_and_core()
    owners = ring_owners(chip, chips) if ringed else range(chips)
    at = 0
    for own_ref, twin_ref in zip(refs[0:-1:2], refs[1:-1:2]):
        for i in range(own_ref.shape[0]):
            out_ref[owners[at], mine] = own_ref[i]
            out_ref[owners[at], 1 - mine] = twin_ref[i]
            at += 1


def pair_rows(pairs, chips, ringed):
    rows, columns = pairs[0][0].shape[1:]
    flat = [p for pair in pairs for p in pair]
    return pl.pallas_call(
        functools.partial(pair_rows_kernel, chips, ringed),
        out_shape=jax.ShapeDtypeStruct((chips, 2, rows, columns), BF16),
        in_specs=[whole()] * len(flat),
        out_specs=whole(),
        compiler_params=params(),
        name="pair_rows",
    )(*flat)


def weave_kernel(own_ref, other_ref, out_ref):
    _, core = chip_and_core()
    chips, rows, columns = own_ref.shape
    for c in range(chips):
        own, other = own_ref[c], other_ref[c]
        out_ref[2 * c * rows : (2 * c + 1) * rows, :] = jnp.where(core == 0, own, other)
        out_ref[(2 * c + 1) * rows : (2 * c + 2) * rows, :] = jnp.where(core == 0, other, own)


def weave(own, other):
    chips, two, rows, columns = own.shape
    own, other = (x.reshape(chips, two * rows, columns) for x in (own, other))
    return pl.pallas_call(
        weave_kernel,
        out_shape=jax.ShapeDtypeStruct((4 * chips * rows, columns), BF16),
        in_specs=[whole()] * 2,
        out_specs=whole(),
        compiler_params=params(),
        name="weave",
    )(own, other)


def shard_blocks(owner, core):
    first = (owner * 2 + core) * (TOK_DEV // BLOCK)
    return [first + u for u in range(TOK_DEV // BLOCK)]


def absorb(pair_ref, kv_all, owners, core):
    blocks = TOK_DEV // BLOCK
    for t, owner in enumerate(owners):
        for u, block in enumerate(shard_blocks(owner, core)):
            kv_all[block] = pair_ref[t * blocks + u]


def project_kernel(chips, starts, width, shards, before, *refs):
    n = len(starts)
    inputs, (gain_ref, weight_ref), (q_all, kv_all, pair_ref) = refs[:n], refs[n : n + 2], refs[-3:]
    chip, core = chip_and_core()
    owners = ring_owners(chip, chips)
    places = [(ref, at) for ref, spots in zip(inputs, starts) for at in spots]
    for begin in range(0, len(places), CHUNK):
        segments = [ref[at : at + BLOCK, :] for ref, at in places[begin : begin + CHUNK]]
        normed = layer_norm(jnp.concatenate(segments, axis=0), gain_ref[...])
        result = jnp.dot(normed, weight_ref[...], preferred_element_type=F32)
        for j in range(len(segments)):
            i = begin + j
            rows = result[j * BLOCK : (j + 1) * BLOCK]
            t, u = divmod(i, TOK_DEV // BLOCK)
            q_all[owners[shards[t]] * (TOK_DEV // BLOCK) + u] = rows[:, :width].astype(BF16)
            pair_ref[i, 0, :, :width] = rows[:, width : 2 * width].astype(BF16)
            pair_ref[i, 1, :width, :] = jnp.transpose(rows[:, 2 * width :]).astype(BF16)
            if width < BLOCK:
                pair_ref[i, 0, :, width:] = jnp.zeros((BLOCK, BLOCK - width), BF16)
                pair_ref[i, 1, width:, :] = jnp.zeros((BLOCK - width, BLOCK), BF16)
    absorb(pair_ref, kv_all, [owners[s] for s in shards], core)
    for i, held in enumerate(before):
        absorb(refs[n + 4 + i], kv_all, [owners[s] for s in held], 1 - core)


def project(pieces, starts, gain, weight, width, chips, shards, before, state):
    blocks = sum(len(s) for s in starts)
    n = len(pieces)
    total = chips * (TOK_DEV // BLOCK)
    return pl.pallas_call(
        functools.partial(project_kernel, chips, starts, width, shards, before),
        out_shape=(
            jax.ShapeDtypeStruct((total, BLOCK, width), BF16),
            jax.ShapeDtypeStruct((2 * total, 2, BLOCK, BLOCK), BF16),
            jax.ShapeDtypeStruct((blocks, 2, BLOCK, BLOCK), BF16),
        ),
        in_specs=[whole()] * (n + 2 + len(state)),
        out_specs=(whole(),) * 3,
        input_output_aliases={n + 2: 0, n + 3: 1} if state else {},
        compiler_params=params(),
        name="project",
    )(*pieces, gain, weight, *state)


def attend_kernel(chips, group, heads, steps, last, lists_ref, counts_ref, q_all, *refs):
    width = heads * HEAD_DIM
    outs, mixed = refs[-1 - len(steps) : -1], refs[-1]
    chip, core = chip_and_core()
    kv_all = refs[0]
    if last:
        kv_all = refs[1 + len(last)]
        owners = ring_owners(chip, chips)
        for i, held in enumerate(last):
            absorb(refs[1 + i], kv_all, [owners[s] for s in held], 1 - core)
    member = lax.rem(chip, group)
    blocks = TOK_DEV // BLOCK
    per_piece = blocks // group

    def place_of(index):
        target = lax.bitwise_xor(chip, steps[0] + lax.div(index, per_piece))
        within = member * per_piece + lax.rem(index, per_piece)
        return target * blocks + within, (target * 2 + core) * blocks + within

    def attend_block(index, used):
        row, block = place_of(index)
        count = counts_ref[block]
        picked = [lists_ref[s, block] for s in range(used)]
        stacked = head_masked(q_all[row], heads)
        scores = []
        for s, p in enumerate(picked):
            one = lax.dot_general(
                kv_all[p, 0][:, :width], stacked, NT, preferred_element_type=F32
            )
            if s:
                one = one + jnp.where(s < count, 0.0, -jnp.inf).astype(F32)
            scores.append(one)
        scores = jnp.concatenate(scores, axis=0)
        top = jnp.max(scores, axis=0, keepdims=True)
        weights = jnp.exp2((scores - top) * EXP2_SCALE)
        total = jnp.sum(weights, axis=0, keepdims=True)
        values = jnp.concatenate([kv_all[p, 1] for p in picked], axis=1)[:width]
        full = jnp.dot(values, weights.astype(BF16), preferred_element_type=F32)
        full = full * (1.0 / total)
        result = jnp.concatenate(
            [
                full[h * HEAD_DIM : (h + 1) * HEAD_DIM, h * BLOCK : (h + 1) * BLOCK]
                for h in range(heads)
            ],
            axis=0,
        )
        return jnp.transpose(result).astype(BF16)

    def one_pair(pair, carry):
        first, second = 2 * pair, 2 * pair + 1
        most = jnp.maximum(counts_ref[place_of(first)[1]], counts_ref[place_of(second)[1]])
        for used in range(1, MAXK + 1):

            @pl.when(most == used)
            def _(used=used):
                one, two = attend_block(first, used), attend_block(second, used)
                mixed[first] = one
                mixed[second] = two

        return carry

    lax.fori_loop(0, len(steps) * per_piece // 2, one_pair, 0)
    for k in range(len(steps)):
        for part in range(per_piece):
            outs[k][part * BLOCK : (part + 1) * BLOCK, :] = mixed[k * per_piece + part]


def attend(lists, counts, q_all, kv_all, extra, chips, group, heads, steps, last):
    width = heads * HEAD_DIM
    piece = TOK_DEV // group
    kv_shape = [jax.ShapeDtypeStruct(kv_all.shape, BF16)] if last else []
    return pl.pallas_call(
        functools.partial(attend_kernel, chips, group, heads, steps, last),
        out_shape=kv_shape + [jax.ShapeDtypeStruct((piece, width), BF16)] * len(steps),
        in_specs=[scalars()] * 2 + [whole()] * (2 + len(extra)),
        out_specs=[whole()] * (len(kv_shape) + len(steps)),
        input_output_aliases={3: 0} if last else {},
        scratch_shapes=[pltpu.VMEM((len(steps) * (piece // BLOCK), BLOCK, width), BF16)],
        compiler_params=params(),
        name="attend",
    )(lists, counts, q_all, kv_all, *extra)


def tail_kernel(chips, group, heads, split, parts, *refs):
    width = heads * HEAD_DIM
    sets = HEADS // heads
    piece = TOK_DEV // group
    got = refs[:chips]
    tokens_ref, gain_ref, probe_ref, *weight_refs = refs[chips : chips + 3 + parts]
    layer_ref, *part_refs, stage = refs[chips + 3 + parts :]
    chip, core = chip_and_core()
    for k in range(chips):
        source = lax.bitwise_xor(chip, k)
        if group == 1:
            stage[source] = got[k][...]
        else:
            stage[source // group, pl.ds(pl.multiple_of(source % group * piece, piece), piece), :] = got[k][...]
    if parts == 1:
        attended = jnp.concatenate([stage[s] for s in range(sets)], axis=1)
        projected = jnp.dot(attended, weight_refs[0][...], preferred_element_type=F32)
    else:
        left = lax.broadcasted_iota(jnp.int32, (TOK_DEV, width), 1) < HEAD_DIM
        ours, theirs = [], []
        for s in range(0, sets, 2):
            one, two = stage[s], stage[s + 1]
            first = jnp.where(left, one, pltpu.roll(two, HEAD_DIM, axis=1))
            second = jnp.where(left, pltpu.roll(one, HEAD_DIM, axis=1), two)
            ours.append(jnp.where(core == 0, first, second))
            theirs.append(jnp.where(core == 0, second, first))
        projected = jnp.dot(
            jnp.concatenate(ours, axis=1), weight_refs[0][...], preferred_element_type=F32
        )
        projected += jnp.dot(
            jnp.concatenate(theirs, axis=1), weight_refs[1][...], preferred_element_type=F32
        )
    layer = (tokens_ref[...].astype(F32) + projected).astype(BF16)
    layer_ref[...] = layer
    pooled = layer_norm(layer, gain_ref[...])
    rows = []

    def emit(lo, value):
        hi = lo + value.shape[1]
        if not split:
            part_refs[0][:, lo:hi] = value.astype(BF16)
            return
        lines, share = chips // 2, PROBES // (2 * chips)
        shaped = value.reshape(lines, 2, 2, share, value.shape[1])
        side = lax.bitwise_and(chip, 1)
        near = jnp.where(side == 0, shaped[:, 0], shaped[:, 1])
        far = jnp.where(side == 0, shaped[:, 1], shaped[:, 0])
        for i, rows_of in enumerate((near, far)):
            mine = jnp.where(core == 0, rows_of[:, 0], rows_of[:, 1])
            theirs = jnp.where(core == 0, rows_of[:, 1], rows_of[:, 0])
            part_refs[2 * i][:, lo:hi] = mine.reshape(lines * share, -1).astype(BF16)
            part_refs[2 * i + 1][:, lo:hi] = theirs.reshape(lines * share, -1).astype(BF16)

    for pair in range(HEADS // 2):
        lo = pair * 2 * HEAD_DIM
        own = pooled[:, lo : lo + 2 * HEAD_DIM]
        stacked = head_masked(probe_ref[:, lo : lo + 2 * HEAD_DIM], 2)
        scores = lax.dot_general(own, stacked, NT, preferred_element_type=F32)
        top = jnp.max(scores, axis=0, keepdims=True)
        weights = jnp.exp2((scores - top) * EXP2_SCALE)
        total = jnp.sum(weights, axis=0, keepdims=True)
        flipped = jnp.transpose(own.astype(F32)).astype(BF16)
        full = jnp.dot(flipped, weights.astype(BF16), preferred_element_type=F32) / total
        result = jnp.concatenate([full[:HEAD_DIM, :PROBES], full[HEAD_DIM:, PROBES:]], axis=0)
        emit(lo, jnp.transpose(result))
        logs = top * SCALE + jnp.log(total)
        rows += [logs[:, :PROBES], logs[:, PROBES:]]
    logs = jnp.concatenate(rows, axis=0)
    high = logs.astype(BF16).astype(F32)
    middle = (logs - high).astype(BF16).astype(F32)
    low = logs - high - middle
    rest = jnp.zeros((STATS - 3 * HEADS, PROBES), F32)
    emit(D, jnp.transpose(jnp.concatenate([high, middle, low, rest], axis=0)))


def tail(got, weights, tokens, gain, probes, chips, group, heads, split):
    width = heads * HEAD_DIM
    rows = PROBES // 4 if split else PROBES
    return pl.pallas_call(
        functools.partial(tail_kernel, chips, group, heads, split, len(weights)),
        out_shape=[jax.ShapeDtypeStruct((TOK_DEV, D), BF16)]
        + [jax.ShapeDtypeStruct((rows, D + STATS), BF16)] * (4 if split else 1),
        in_specs=[whole()] * (chips + 3 + len(weights)),
        out_specs=[whole()] * (5 if split else 2),
        scratch_shapes=[pltpu.VMEM((HEADS // heads, TOK_DEV, width), BF16)],
        compiler_params=params(),
        name="tail",
    )(*got, tokens, gain, probes, *weights)


def read_logs(block):
    pick = lax.broadcasted_iota(jnp.int32, (STATS, STATS), 0)
    head = lax.broadcasted_iota(jnp.int32, (STATS, STATS), 1)
    gather = ((pick < 3 * HEADS) & (pick % HEADS == head)).astype(BF16)
    return jnp.dot(block, gather, preferred_element_type=F32)


def spread_heads(factors):
    row = lax.broadcasted_iota(jnp.int32, (STATS, D), 0)
    lane = lax.broadcasted_iota(jnp.int32, (STATS, D), 1)
    widen = (lane // HEAD_DIM == row).astype(F32)
    return jnp.dot(factors, widen, preferred_element_type=F32, precision=lax.Precision.HIGHEST)


def blend(blocks):
    logs = [read_logs(b[:, D:]) for b in blocks]
    top = functools.reduce(jnp.maximum, logs)
    shares = [jnp.exp(one - top) for one in logs]
    total = functools.reduce(jnp.add, shares)
    rows = blocks[0].shape[0]
    wide = spread_heads(jnp.concatenate([s / total for s in shares], axis=0))
    value = 0.0
    for i, b in enumerate(blocks):
        value = value + wide[i * rows : (i + 1) * rows] * b[:, :D].astype(F32)
    return value, top + jnp.log(total)


def repack(value, logs):
    high = logs.astype(BF16).astype(F32)
    middle = (logs - high).astype(BF16).astype(F32)
    low = logs - high - middle
    rest = jnp.zeros((value.shape[0], STATS - 3 * HEADS), F32)
    return jnp.concatenate(
        [value, high[:, :HEADS], middle[:, :HEADS], low[:, :HEADS], rest], axis=1
    ).astype(BF16)


def deal_kernel(count, *refs):
    outs, stage = refs[count:-1], refs[-1]
    chip, _ = chip_and_core()
    line = lax.shift_right_logical(chip, 1)
    packed = repack(*blend([ref[...] for ref in refs[:count]]))
    stage[...] = packed.reshape(stage.shape)
    for k in range(len(outs)):
        outs[k][...] = stage[lax.bitwise_xor(line, k)]


def deal(blocks, parts):
    share = blocks[0].shape[0] // parts
    return pl.pallas_call(
        functools.partial(deal_kernel, len(blocks)),
        out_shape=[jax.ShapeDtypeStruct((share, D + STATS), BF16)] * parts,
        in_specs=[whole()] * len(blocks),
        out_specs=[whole()] * parts,
        scratch_shapes=[pltpu.VMEM((parts, share, D + STATS), BF16)],
        compiler_params=params(),
        name="deal",
    )(*blocks)


def last_kernel(*refs):
    refs[-1][...] = blend([r[...] for r in refs[:-1]])[0]


def join(parts):
    return pl.pallas_call(
        last_kernel,
        out_shape=jax.ShapeDtypeStruct((parts[0].shape[0], D), F32),
        in_specs=[whole()] * len(parts),
        out_specs=whole(),
        compiler_params=params(),
        name="join",
    )(*parts)


def per_device(
    tokens,
    ln_gain,
    w_query,
    w_key,
    w_value,
    w_out,
    probe_gain,
    probe_queries,
    key_blocks,
    key_counts,
):
    ranks = lax.axis_size("seq")
    chips = ranks // 2
    heads = max(1, HEADS // chips)
    group = max(1, chips // HEADS)
    sets = HEADS // heads
    width = heads * HEAD_DIM
    myself = lax.axis_index("seq")
    core = myself % 2
    order = list(range(0, chips, 2)) + list(range(chips - 1, 0, -2))
    swap = [(i, i ^ 1) for i in range(ranks)]
    same_core = [[2 * c + k for c in range(chips)] for k in range(2)]

    def around(shift):
        return [
            (order[i] * 2 + k, order[(i + shift) % chips] * 2 + k)
            for i in range(chips)
            for k in range(2)
        ]

    def across(k):
        return [(2 * c + q, 2 * (c ^ k) + q) for c in range(chips) for q in range(2)]

    twins = [(i, i ^ 1) for i in range(lax.axis_size("scan"))]
    barrier = lax.optimization_barrier
    depth = w_query.shape[0]
    gain = ln_gain.reshape(1, D)
    half = TOK_DEV // 2
    packed = depth == 64 and chips == 8

    if packed:
        load, mine, theirs = prepare(tokens, (w_query, w_key, w_value), w_out, width)
        sent = bundle(mine, lax.ppermute(theirs, "seq", swap))

        def serve(offset):
            pairs = []
            for x in range(lax.axis_size("scan")):
                for rank in range(ranks):
                    flip = 2 * (x & 1) + (rank & 1) + offset
                    if flip:
                        pairs.append((x * ranks + rank, x * ranks + (rank ^ (2 * flip))))
            return pairs

        moved = [lax.ppermute(sent[j], ("scan", "seq"), serve(4 * j)) for j in range(2)]
    else:
        columns = jnp.stack([w_query, w_key, w_value]).reshape(3, depth, sets, width)
        columns = jnp.transpose(columns, (2, 1, 0, 3)).reshape(sets, depth, 3 * width)
        columns = jnp.repeat(columns, group, axis=0)
        here = lax.all_to_all(
            columns, "seq", split_axis=0, concat_axis=0, tiled=True, axis_index_groups=same_core
        )
        there = lax.ppermute(here, "seq", swap)
        even = jnp.where(core == 0, here, there)
        odd = jnp.where(core == 0, there, here)
        weight = jnp.stack([even, odd], axis=1).reshape(D, 3 * width)
        out_weights = [lax.all_gather(w_out, "seq", axis=0, tiled=True)]

    load = load if packed else tokens
    length = load.shape[0] // 2
    forward = backward = load

    def spread(*shards):
        return [(shard, at) for shard in shards for at in (0, length)]

    state, others = (), []

    def advance(pieces, shards):
        nonlocal state, others
        q_all, kv_all, pair = project(
            [array for array, _ in pieces],
            tuple((at,) for _, at in pieces),
            gain,
            weight,
            width,
            chips,
            shards,
            tuple(held for _, held in others),
            state + tuple(other for other, _ in others),
        )
        state, others = (q_all, kv_all), []
        return pair

    def send(pair, shards):
        others.append((lax.ppermute(pair, "seq", swap), shards))

    arrived, shards = spread(load), (0,)
    for s in range(1, chips // 2 - 1):
        forward = lax.ppermute(forward, "seq", around(1))
        backward = lax.ppermute(backward, "seq", around(-1))
        if packed and s == 1:
            forward, backward, *moved = barrier((forward, backward, *moved))
        if packed and s == 2:
            blocks = keep(sent[0], *moved)
            twin_blocks = lax.ppermute(blocks, "scan", twins)
            joint = gather_blocks(
                [(blocks, 0), (blocks, 1), (twin_blocks, 0), (twin_blocks, 1)], False
            )
            weight = assemble(blocks, twin_blocks, lax.ppermute(joint, "seq", swap))
            forward, backward, weight = barrier((forward, backward, weight))
        arrived += spread(forward, backward)
        shards += (2 * s - 1, 2 * s)
    if packed:
        early = collect(arrived, depth // 2)
        early_twin = lax.ppermute(early, "scan", twins)
        weight, early_twin = barrier((weight, early_twin))
    pair = advance(arrived, shards)
    forward = lax.ppermute(forward, "seq", around(1))
    backward = lax.ppermute(backward, "seq", around(-1))
    forward, backward, pair, *state = barrier((forward, backward, pair, *state))
    state = tuple(state)
    final = (
        lax.ppermute(forward[:length], "seq", around(1)),
        lax.ppermute(backward[length:], "seq", around(-1)),
    )
    if packed:
        middle = collect(spread(forward, backward), depth // 2)
        middle_twin = lax.ppermute(middle, "scan", twins)
        q_all, kv_all, middle_twin = barrier((*state, middle_twin))
        state = (q_all, kv_all)
    near_shards = (chips - 3, chips - 2)
    near = advance(spread(forward, backward), near_shards)
    pair, near, *final = barrier((pair, near, *final))
    send(pair, shards)
    send(near, near_shards)
    held, others = others, []
    last = [(array, 0) for array in final]
    send(advance(last, (chips - 1,)), (chips - 1,))
    others = held + others
    if packed:
        late = collect(last, depth // 2)
        late_twin = lax.ppermute(late, "scan", twins)
    q_all, kv_all = state
    attended = attend(
        key_blocks.T,
        key_counts,
        q_all,
        kv_all,
        [other for other, _ in others],
        chips,
        group,
        heads,
        tuple(range(chips)),
        tuple(held for _, held in others),
    )[1:]
    if packed:
        first, middle_twin, late_twin = barrier((attended[0], middle_twin, late_twin))
        attended = [first, *attended[1:]]
        own_half = pair_rows(
            [(early, early_twin), (middle, middle_twin), (late, late_twin)], chips, True
        )
        other_half = lax.ppermute(own_half, "seq", swap)
        out_weights = [half.reshape(D // 2, D) for half in (own_half, other_half)]
    got = [attended[0]] + [lax.ppermute(attended[k], "seq", across(k)) for k in range(1, chips)]

    share = PROBES // ranks
    split = share % 16 == 0
    layer_out, *parts = tail(
        got,
        out_weights,
        tokens,
        probe_gain.reshape(1, D),
        probe_queries,
        chips,
        group,
        heads,
        split,
    )
    if split:
        mine, core_part, side_part, both_part = parts
        blocks = [
            mine,
            lax.ppermute(side_part, "seq", across(1)),
            lax.ppermute(both_part, "seq", [(i, i ^ 3) for i in range(ranks)]),
            lax.ppermute(core_part, "seq", swap),
        ]
        lines = deal(blocks, chips // 2)
        joined = [lines[0]] + [
            lax.ppermute(lines[k], "seq", across(2 * k)) for k in range(1, chips // 2)
        ]
        return layer_out, join(joined)
    rows = lax.all_to_all(
        parts[0].reshape(ranks, share, D + STATS), "seq", split_axis=0, concat_axis=0, tiled=True
    ).astype(F32)
    logs = rows[:, :, D : D + 3 * HEADS].reshape(ranks, share, 3, HEADS).sum(axis=2)
    factors = jnp.exp(logs - jnp.max(logs, axis=0, keepdims=True))
    factors = factors / jnp.sum(factors, axis=0, keepdims=True)
    probe_out = jnp.sum(jnp.repeat(factors, HEAD_DIM, axis=2) * rows[:, :, :D], axis=0)
    return layer_out, probe_out


def solution(mesh):
    return jax.shard_map(
        per_device,
        mesh=mesh,
        in_specs=(
            P(("scan", "seq"), None),
            P(),
            P("seq", None),
            P("seq", None),
            P("seq", None),
            P("seq", None),
            P(),
            P(),
            P("scan", None),
            P("scan"),
        ),
        out_specs=(P(("scan", "seq"), None), P(("scan", "seq"), None)),
        check_vma=False,
    )
```

```python
import functools
import math

import jax
import jax.numpy as jnp
from jax import lax
from jax.experimental import pallas as pl
from jax.experimental.pallas import tpu as pltpu
from jax.sharding import PartitionSpec as P

D = 1024
HEADS = 16
HEAD_DIM = 64
PROBES = 256
BLOCK = 128
MAXK = 8
TOK_DEV = 256
STATS = 128
CHUNK = 4
EPS = 1e-05
SCALE = 1.0 / math.sqrt(HEAD_DIM)
EXP2_SCALE = SCALE / math.log(2.0)
BF16 = jnp.bfloat16
F32 = jnp.float32
NT = (((1,), (1,)), ((), ()))
VMEM_BYTES = 28 * 1024 * 1024


def whole():
    return pl.BlockSpec(memory_space=pltpu.VMEM)


def scalars():
    return pl.BlockSpec(memory_space=pltpu.SMEM)


def params():
    return pltpu.CompilerParams(vmem_limit_bytes=VMEM_BYTES)


def layer_norm(values, gain):
    wide = values.astype(F32)
    center = wide - jnp.mean(wide, axis=-1, keepdims=True)
    spread = jnp.mean(center * center, axis=-1, keepdims=True)
    return (center * lax.rsqrt(spread + EPS) * gain).astype(BF16)


def head_masked(block, heads):
    if heads == 1:
        return block
    lanes = lax.broadcasted_iota(jnp.int32, block.shape, 1) // HEAD_DIM
    zero = jnp.zeros_like(block)
    return jnp.concatenate([jnp.where(lanes == h, block, zero) for h in range(heads)], axis=0)


def chip_and_core():
    rank = lax.axis_index("seq")
    return lax.shift_right_logical(rank, 1), lax.bitwise_and(rank, 1)


def twin():
    return lax.bitwise_and(lax.axis_index("scan"), 1)


def ring_owners(chip, chips):
    half = lax.shift_right_logical(chip, 1)
    position = jnp.where(lax.bitwise_and(chip, 1) == 1, chips - 1 - half, half)
    offsets = [0]
    for s in range(1, chips // 2):
        offsets += [-s, s]
    offsets.append(chips // 2)
    owners = []
    for offset in offsets:
        spot = lax.rem(position + (offset + chips), chips)
        owners.append(jnp.where(spot < chips // 2, 2 * spot, 2 * (chips - 1 - spot) + 1))
    return owners


def prepare_kernel(
    width, tokens_ref, query_ref, key_ref, value_ref, out_ref, load_ref, mine_ref, theirs_ref, rows_ref, sems
):
    chip, core = chip_and_core()
    rows = out_ref.shape[0] // 4
    half = TOK_DEV // 2
    step = half + rows
    copies = []
    for part in range(2):
        start = pl.multiple_of(twin() * (2 * rows) + part * rows, rows)
        to = load_ref.at[part * step : part * step + half, :]
        copies.append((tokens_ref.at[part * half : (part + 1) * half, :], to))
        to = load_ref.at[part * step + half : (part + 1) * step, :]
        copies.append((out_ref.at[pl.ds(start, rows), :], to))
    for i, ref in enumerate((query_ref, key_ref, value_ref)):
        copies.append((ref, rows_ref.at[i]))
    copies = [pltpu.make_async_copy(a, b, sems.at[i]) for i, (a, b) in enumerate(copies)]
    for copy in copies:
        copy.start()
    for copy in copies:
        copy.wait()
    for ref, side in ((mine_ref, core), (theirs_ref, 1 - core)):
        for j in range(2):
            target = lax.bitwise_xor(chip, 2 * twin() + side + 4 * j)
            lanes = pl.ds(pl.multiple_of(target * width, width), width)
            for i in range(3):
                ref[j, :, i * width : (i + 1) * width] = rows_ref[i, :, lanes]


def prepare(tokens, weights, out_weight, width):
    rows = out_weight.shape[0] // 2
    block = jax.ShapeDtypeStruct((2, 2 * rows, 3 * width), BF16)
    return pl.pallas_call(
        functools.partial(prepare_kernel, width),
        out_shape=(jax.ShapeDtypeStruct((TOK_DEV + rows, D), BF16), block, block),
        in_specs=[pl.BlockSpec(memory_space=pltpu.HBM)] * 5,
        out_specs=(whole(),) * 3,
        scratch_shapes=[pltpu.VMEM((3, 2 * rows, D), BF16), pltpu.SemaphoreType.DMA((7,))],
        compiler_params=params(),
        name="prepare",
    )(*(pltpu.with_memory_space_constraint(x, pltpu.HBM) for x in (tokens, *weights, out_weight)))


def bundle_kernel(mine_ref, got_ref, *outs):
    _, core = chip_and_core()
    rows = mine_ref.shape[1]
    for j, ref in enumerate(outs):
        mine, got = mine_ref[j], got_ref[j]
        ref[:rows, :] = jnp.where(core == 0, mine, got)
        ref[rows:, :] = jnp.where(core == 0, got, mine)


def bundle(mine, got):
    _, rows, columns = mine.shape
    return pl.pallas_call(
        bundle_kernel,
        out_shape=[jax.ShapeDtypeStruct((2 * rows, columns), BF16)] * 2,
        in_specs=[whole()] * 2,
        out_specs=[whole()] * 2,
        compiler_params=params(),
        name="bundle",
    )(mine, got)


def keep_kernel(own_ref, near_ref, far_ref, out_ref):
    _, core = chip_and_core()
    out_ref[0] = jnp.where(2 * twin() + core == 0, own_ref[...], near_ref[...])
    out_ref[1] = far_ref[...]


def keep(own, near, far):
    return pl.pallas_call(
        keep_kernel,
        out_shape=jax.ShapeDtypeStruct((2,) + own.shape, BF16),
        in_specs=[whole()] * 3,
        out_specs=whole(),
        compiler_params=params(),
        name="keep",
    )(own, near, far)


def assemble_kernel(own_ref, twin_ref, other_ref, out_ref, stage):
    chip, core = chip_and_core()
    role = 2 * twin() + core
    for j in range(2):
        for flip, block in (
            (0, own_ref[j]),
            (2, twin_ref[j]),
            (1, other_ref[j]),
            (3, other_ref[2 + j]),
        ):
            source = lax.bitwise_xor(chip, lax.bitwise_xor(role, flip) + 4 * j)
            stage[source] = block
    out_ref[...] = stage[...].reshape(out_ref.shape)


def assemble(own, twin_blocks, other):
    _, rows, columns = own.shape
    return pl.pallas_call(
        assemble_kernel,
        out_shape=jax.ShapeDtypeStruct((8 * rows, columns), BF16),
        in_specs=[whole()] * 3,
        out_specs=whole(),
        scratch_shapes=[pltpu.VMEM((8, rows, columns), BF16)],
        compiler_params=params(),
        name="assemble",
    )(own, twin_blocks, other)


def gather_blocks_kernel(picks, ordered, *refs):
    chip, _ = chip_and_core()
    for at, (i, j) in enumerate(picks):
        refs[-1][lax.bitwise_xor(chip, at) if ordered else at] = refs[i][j]


def gather_blocks(blocks, ordered):
    arrays, picks = [], []
    for array, j in blocks:
        if not any(array is one for one in arrays):
            arrays.append(array)
        picks.append(([array is one for one in arrays].index(True), j))
    return pl.pallas_call(
        functools.partial(gather_blocks_kernel, tuple(picks), ordered),
        out_shape=jax.ShapeDtypeStruct((len(blocks),) + arrays[0].shape[1:], BF16),
        in_specs=[whole()] * len(arrays),
        out_specs=whole(),
        compiler_params=params(),
        name="gather_blocks",
    )(*arrays)


def collect_kernel(places, *refs):
    out_ref = refs[-1]
    rows = out_ref.shape[1] // 2
    for i, at in enumerate(places):
        part = i % 2
        out_ref[i // 2, part * rows : (part + 1) * rows, :] = refs[i][at : at + rows, :]


def collect(pieces, rows):
    places = tuple(at + TOK_DEV // 2 for _, at in pieces)
    return pl.pallas_call(
        functools.partial(collect_kernel, places),
        out_shape=jax.ShapeDtypeStruct((len(pieces) // 2, rows, D), BF16),
        in_specs=[whole()] * len(pieces),
        out_specs=whole(),
        compiler_params=params(),
        name="collect",
    )(*(array for array, _ in pieces))


def pair_rows_kernel(chips, ringed, *refs):
    out_ref = refs[-1]
    mine = twin()
    chip, _ = chip_and_core()
    owners = ring_owners(chip, chips) if ringed else range(chips)
    at = 0
    for own_ref, twin_ref in zip(refs[0:-1:2], refs[1:-1:2]):
        for i in range(own_ref.shape[0]):
            out_ref[owners[at], mine] = own_ref[i]
            out_ref[owners[at], 1 - mine] = twin_ref[i]
            at += 1


def pair_rows(pairs, chips, ringed):
    rows, columns = pairs[0][0].shape[1:]
    flat = [p for pair in pairs for p in pair]
    return pl.pallas_call(
        functools.partial(pair_rows_kernel, chips, ringed),
        out_shape=jax.ShapeDtypeStruct((chips, 2, rows, columns), BF16),
        in_specs=[whole()] * len(flat),
        out_specs=whole(),
        compiler_params=params(),
        name="pair_rows",
    )(*flat)


def weave_kernel(own_ref, other_ref, out_ref):
    _, core = chip_and_core()
    chips, rows, columns = own_ref.shape
    for c in range(chips):
        own, other = own_ref[c], other_ref[c]
        out_ref[2 * c * rows : (2 * c + 1) * rows, :] = jnp.where(core == 0, own, other)
        out_ref[(2 * c + 1) * rows : (2 * c + 2) * rows, :] = jnp.where(core == 0, other, own)


def weave(own, other):
    chips, two, rows, columns = own.shape
    own, other = (x.reshape(chips, two * rows, columns) for x in (own, other))
    return pl.pallas_call(
        weave_kernel,
        out_shape=jax.ShapeDtypeStruct((4 * chips * rows, columns), BF16),
        in_specs=[whole()] * 2,
        out_specs=whole(),
        compiler_params=params(),
        name="weave",
    )(own, other)


def shard_blocks(owner, core):
    first = (owner * 2 + core) * (TOK_DEV // BLOCK)
    return [first + u for u in range(TOK_DEV // BLOCK)]


def absorb(pair_ref, kv_all, owners, core):
    blocks = TOK_DEV // BLOCK
    for t, owner in enumerate(owners):
        for u, block in enumerate(shard_blocks(owner, core)):
            kv_all[block] = pair_ref[t * blocks + u]


def project_kernel(chips, starts, width, shards, before, *refs):
    n = len(starts)
    inputs, (gain_ref, weight_ref), (q_all, kv_all, pair_ref) = refs[:n], refs[n : n + 2], refs[-3:]
    chip, core = chip_and_core()
    owners = ring_owners(chip, chips)
    places = [(ref, at) for ref, spots in zip(inputs, starts) for at in spots]
    for begin in range(0, len(places), CHUNK):
        segments = [ref[at : at + BLOCK, :] for ref, at in places[begin : begin + CHUNK]]
        normed = layer_norm(jnp.concatenate(segments, axis=0), gain_ref[...])
        result = jnp.dot(normed, weight_ref[...], preferred_element_type=F32)
        for j in range(len(segments)):
            i = begin + j
            rows = result[j * BLOCK : (j + 1) * BLOCK]
            t, u = divmod(i, TOK_DEV // BLOCK)
            q_all[owners[shards[t]] * (TOK_DEV // BLOCK) + u] = rows[:, :width].astype(BF16)
            pair_ref[i, 0, :, :width] = rows[:, width : 2 * width].astype(BF16)
            pair_ref[i, 1, :width, :] = jnp.transpose(rows[:, 2 * width :]).astype(BF16)
            if width < BLOCK:
                pair_ref[i, 0, :, width:] = jnp.zeros((BLOCK, BLOCK - width), BF16)
                pair_ref[i, 1, width:, :] = jnp.zeros((BLOCK - width, BLOCK), BF16)
    absorb(pair_ref, kv_all, [owners[s] for s in shards], core)
    for i, held in enumerate(before):
        absorb(refs[n + 4 + i], kv_all, [owners[s] for s in held], 1 - core)


def project(pieces, starts, gain, weight, width, chips, shards, before, state):
    blocks = sum(len(s) for s in starts)
    n = len(pieces)
    total = chips * (TOK_DEV // BLOCK)
    return pl.pallas_call(
        functools.partial(project_kernel, chips, starts, width, shards, before),
        out_shape=(
            jax.ShapeDtypeStruct((total, BLOCK, width), BF16),
            jax.ShapeDtypeStruct((2 * total, 2, BLOCK, BLOCK), BF16),
            jax.ShapeDtypeStruct((blocks, 2, BLOCK, BLOCK), BF16),
        ),
        in_specs=[whole()] * (n + 2 + len(state)),
        out_specs=(whole(),) * 3,
        input_output_aliases={n + 2: 0, n + 3: 1} if state else {},
        compiler_params=params(),
        name="project",
    )(*pieces, gain, weight, *state)


def attend_kernel(chips, group, heads, steps, last, lists_ref, counts_ref, q_all, *refs):
    width = heads * HEAD_DIM
    outs, mixed = refs[-1 - len(steps) : -1], refs[-1]
    chip, core = chip_and_core()
    kv_all = refs[0]
    if last:
        kv_all = refs[1 + len(last)]
        owners = ring_owners(chip, chips)
        for i, held in enumerate(last):
            absorb(refs[1 + i], kv_all, [owners[s] for s in held], 1 - core)
    member = lax.rem(chip, group)
    blocks = TOK_DEV // BLOCK
    per_piece = blocks // group

    def place_of(index):
        target = lax.bitwise_xor(chip, steps[0] + lax.div(index, per_piece))
        within = member * per_piece + lax.rem(index, per_piece)
        return target * blocks + within, (target * 2 + core) * blocks + within

    def attend_block(index, used):
        row, block = place_of(index)
        count = counts_ref[block]
        picked = [lists_ref[s, block] for s in range(used)]
        stacked = head_masked(q_all[row], heads)
        scores = []
        for s, p in enumerate(picked):
            one = lax.dot_general(
                kv_all[p, 0][:, :width], stacked, NT, preferred_element_type=F32
            )
            if s:
                one = one + jnp.where(s < count, 0.0, -jnp.inf).astype(F32)
            scores.append(one)
        scores = jnp.concatenate(scores, axis=0)
        top = jnp.max(scores, axis=0, keepdims=True)
        weights = jnp.exp2((scores - top) * EXP2_SCALE)
        values = jnp.concatenate([kv_all[p, 1] for p in picked], axis=1)[:width]
        values = jnp.concatenate([values, jnp.ones((16, used * BLOCK), BF16)], axis=0)
        full = jnp.dot(values, weights.astype(BF16), preferred_element_type=F32)
        full = full[:width] * (1.0 / full[width : width + 1])
        result = jnp.concatenate(
            [
                full[h * HEAD_DIM : (h + 1) * HEAD_DIM, h * BLOCK : (h + 1) * BLOCK]
                for h in range(heads)
            ],
            axis=0,
        )
        return jnp.transpose(result).astype(BF16)

    def one_pair(pair, carry):
        first, second = 2 * pair, 2 * pair + 1
        most = jnp.maximum(counts_ref[place_of(first)[1]], counts_ref[place_of(second)[1]])
        for used in range(1, MAXK + 1):

            @pl.when(most == used)
            def _(used=used):
                one, two = attend_block(first, used), attend_block(second, used)
                mixed[first] = one
                mixed[second] = two

        return carry

    lax.fori_loop(0, len(steps) * per_piece // 2, one_pair, 0)
    for k in range(len(steps)):
        for part in range(per_piece):
            outs[k][part * BLOCK : (part + 1) * BLOCK, :] = mixed[k * per_piece + part]


def attend(lists, counts, q_all, kv_all, extra, chips, group, heads, steps, last):
    width = heads * HEAD_DIM
    piece = TOK_DEV // group
    kv_shape = [jax.ShapeDtypeStruct(kv_all.shape, BF16)] if last else []
    return pl.pallas_call(
        functools.partial(attend_kernel, chips, group, heads, steps, last),
        out_shape=kv_shape + [jax.ShapeDtypeStruct((piece, width), BF16)] * len(steps),
        in_specs=[scalars()] * 2 + [whole()] * (2 + len(extra)),
        out_specs=[whole()] * (len(kv_shape) + len(steps)),
        input_output_aliases={3: 0} if last else {},
        scratch_shapes=[pltpu.VMEM((len(steps) * (piece // BLOCK), BLOCK, width), BF16)],
        compiler_params=params(),
        name="attend",
    )(lists, counts, q_all, kv_all, *extra)


def tail_kernel(chips, group, heads, split, parts, *refs):
    width = heads * HEAD_DIM
    sets = HEADS // heads
    piece = TOK_DEV // group
    got = refs[:chips]
    tokens_ref, gain_ref, probe_ref, *weight_refs = refs[chips : chips + 3 + parts]
    layer_ref, *part_refs, stage = refs[chips + 3 + parts :]
    chip, core = chip_and_core()
    for k in range(chips):
        source = lax.bitwise_xor(chip, k)
        if group == 1:
            stage[source] = got[k][...]
        else:
            stage[source // group, pl.ds(pl.multiple_of(source % group * piece, piece), piece), :] = got[k][...]
    if parts == 1:
        attended = jnp.concatenate([stage[s] for s in range(sets)], axis=1)
        projected = jnp.dot(attended, weight_refs[0][...], preferred_element_type=F32)
    else:
        left = lax.broadcasted_iota(jnp.int32, (TOK_DEV, width), 1) < HEAD_DIM
        ours, theirs = [], []
        for s in range(0, sets, 2):
            one, two = stage[s], stage[s + 1]
            first = jnp.where(left, one, pltpu.roll(two, HEAD_DIM, axis=1))
            second = jnp.where(left, pltpu.roll(one, HEAD_DIM, axis=1), two)
            ours.append(jnp.where(core == 0, first, second))
            theirs.append(jnp.where(core == 0, second, first))
        projected = jnp.dot(
            jnp.concatenate(ours, axis=1), weight_refs[0][...], preferred_element_type=F32
        )
        projected += jnp.dot(
            jnp.concatenate(theirs, axis=1), weight_refs[1][...], preferred_element_type=F32
        )
    layer = (tokens_ref[...].astype(F32) + projected).astype(BF16)
    layer_ref[...] = layer
    pooled = layer_norm(layer, gain_ref[...])
    rows = []

    def emit(lo, value):
        hi = lo + value.shape[1]
        if not split:
            part_refs[0][:, lo:hi] = value.astype(BF16)
            return
        lines, share = chips // 2, PROBES // (2 * chips)
        shaped = value.reshape(lines, 2, 2, share, value.shape[1])
        side = lax.bitwise_and(chip, 1)
        near = jnp.where(side == 0, shaped[:, 0], shaped[:, 1])
        far = jnp.where(side == 0, shaped[:, 1], shaped[:, 0])
        for i, rows_of in enumerate((near, far)):
            mine = jnp.where(core == 0, rows_of[:, 0], rows_of[:, 1])
            theirs = jnp.where(core == 0, rows_of[:, 1], rows_of[:, 0])
            part_refs[2 * i][:, lo:hi] = mine.reshape(lines * share, -1).astype(BF16)
            part_refs[2 * i + 1][:, lo:hi] = theirs.reshape(lines * share, -1).astype(BF16)

    for pair in range(HEADS // 2):
        lo = pair * 2 * HEAD_DIM
        own = pooled[:, lo : lo + 2 * HEAD_DIM]
        stacked = head_masked(probe_ref[:, lo : lo + 2 * HEAD_DIM], 2)
        scores = lax.dot_general(own, stacked, NT, preferred_element_type=F32)
        top = jnp.max(scores, axis=0, keepdims=True)
        weights = jnp.exp2((scores - top) * EXP2_SCALE)
        flipped = jnp.transpose(own.astype(F32)).astype(BF16)
        flipped = jnp.concatenate([flipped, jnp.ones((16, TOK_DEV), BF16)], axis=0)
        full = jnp.dot(flipped, weights.astype(BF16), preferred_element_type=F32)
        total = full[2 * HEAD_DIM : 2 * HEAD_DIM + 1]
        full = full[: 2 * HEAD_DIM] * (1.0 / total)
        result = jnp.concatenate([full[:HEAD_DIM, :PROBES], full[HEAD_DIM:, PROBES:]], axis=0)
        emit(lo, jnp.transpose(result))
        logs = top * SCALE + jnp.log(total)
        rows += [logs[:, :PROBES], logs[:, PROBES:]]
    logs = jnp.concatenate(rows, axis=0)
    high = logs.astype(BF16).astype(F32)
    middle = (logs - high).astype(BF16).astype(F32)
    low = logs - high - middle
    rest = jnp.zeros((STATS - 3 * HEADS, PROBES), F32)
    emit(D, jnp.transpose(jnp.concatenate([high, middle, low, rest], axis=0)))


def tail(got, weights, tokens, gain, probes, chips, group, heads, split):
    width = heads * HEAD_DIM
    rows = PROBES // 4 if split else PROBES
    return pl.pallas_call(
        functools.partial(tail_kernel, chips, group, heads, split, len(weights)),
        out_shape=[jax.ShapeDtypeStruct((TOK_DEV, D), BF16)]
        + [jax.ShapeDtypeStruct((rows, D + STATS), BF16)] * (4 if split else 1),
        in_specs=[whole()] * (chips + 3 + len(weights)),
        out_specs=[whole()] * (5 if split else 2),
        scratch_shapes=[pltpu.VMEM((HEADS // heads, TOK_DEV, width), BF16)],
        compiler_params=params(),
        name="tail",
    )(*got, tokens, gain, probes, *weights)


def read_logs(block):
    pick = lax.broadcasted_iota(jnp.int32, (STATS, STATS), 0)
    head = lax.broadcasted_iota(jnp.int32, (STATS, STATS), 1)
    gather = ((pick < 3 * HEADS) & (pick % HEADS == head)).astype(BF16)
    return jnp.dot(block, gather, preferred_element_type=F32)


def spread_heads(factors):
    row = lax.broadcasted_iota(jnp.int32, (STATS, D), 0)
    lane = lax.broadcasted_iota(jnp.int32, (STATS, D), 1)
    widen = (lane // HEAD_DIM == row).astype(F32)
    return jnp.dot(factors, widen, preferred_element_type=F32, precision=lax.Precision.HIGHEST)


def blend(blocks):
    logs = [read_logs(b[:, D:]) for b in blocks]
    top = functools.reduce(jnp.maximum, logs)
    shares = [jnp.exp(one - top) for one in logs]
    total = functools.reduce(jnp.add, shares)
    rows = blocks[0].shape[0]
    wide = spread_heads(jnp.concatenate([s / total for s in shares], axis=0))
    value = 0.0
    for i, b in enumerate(blocks):
        value = value + wide[i * rows : (i + 1) * rows] * b[:, :D].astype(F32)
    return value, top + jnp.log(total)


def repack(value, logs):
    high = logs.astype(BF16).astype(F32)
    middle = (logs - high).astype(BF16).astype(F32)
    low = logs - high - middle
    rest = jnp.zeros((value.shape[0], STATS - 3 * HEADS), F32)
    return jnp.concatenate(
        [value, high[:, :HEADS], middle[:, :HEADS], low[:, :HEADS], rest], axis=1
    ).astype(BF16)


def deal_kernel(count, *refs):
    outs, stage = refs[count:-1], refs[-1]
    chip, _ = chip_and_core()
    line = lax.shift_right_logical(chip, 1)
    packed = repack(*blend([ref[...] for ref in refs[:count]]))
    stage[...] = packed.reshape(stage.shape)
    for k in range(len(outs)):
        outs[k][...] = stage[lax.bitwise_xor(line, k)]


def deal(blocks, parts):
    share = blocks[0].shape[0] // parts
    return pl.pallas_call(
        functools.partial(deal_kernel, len(blocks)),
        out_shape=[jax.ShapeDtypeStruct((share, D + STATS), BF16)] * parts,
        in_specs=[whole()] * len(blocks),
        out_specs=[whole()] * parts,
        scratch_shapes=[pltpu.VMEM((parts, share, D + STATS), BF16)],
        compiler_params=params(),
        name="deal",
    )(*blocks)


def last_kernel(*refs):
    refs[-1][...] = blend([r[...] for r in refs[:-1]])[0]


def join(parts):
    return pl.pallas_call(
        last_kernel,
        out_shape=jax.ShapeDtypeStruct((parts[0].shape[0], D), F32),
        in_specs=[whole()] * len(parts),
        out_specs=whole(),
        compiler_params=params(),
        name="join",
    )(*parts)


def per_device(
    tokens,
    ln_gain,
    w_query,
    w_key,
    w_value,
    w_out,
    probe_gain,
    probe_queries,
    key_blocks,
    key_counts,
):
    ranks = lax.axis_size("seq")
    chips = ranks // 2
    heads = max(1, HEADS // chips)
    group = max(1, chips // HEADS)
    sets = HEADS // heads
    width = heads * HEAD_DIM
    myself = lax.axis_index("seq")
    core = myself % 2
    order = list(range(0, chips, 2)) + list(range(chips - 1, 0, -2))
    swap = [(i, i ^ 1) for i in range(ranks)]
    same_core = [[2 * c + k for c in range(chips)] for k in range(2)]

    def around(shift):
        return [
            (order[i] * 2 + k, order[(i + shift) % chips] * 2 + k)
            for i in range(chips)
            for k in range(2)
        ]

    def across(k):
        return [(2 * c + q, 2 * (c ^ k) + q) for c in range(chips) for q in range(2)]

    twins = [(i, i ^ 1) for i in range(lax.axis_size("scan"))]
    barrier = lax.optimization_barrier
    depth = w_query.shape[0]
    gain = ln_gain.reshape(1, D)
    half = TOK_DEV // 2
    packed = depth == 64 and chips == 8

    if packed:
        load, mine, theirs = prepare(tokens, (w_query, w_key, w_value), w_out, width)
        sent = bundle(mine, lax.ppermute(theirs, "seq", swap))

        def serve(offset):
            pairs = []
            for x in range(lax.axis_size("scan")):
                for rank in range(ranks):
                    flip = 2 * (x & 1) + (rank & 1) + offset
                    if flip:
                        pairs.append((x * ranks + rank, x * ranks + (rank ^ (2 * flip))))
            return pairs

        moved = [lax.ppermute(sent[j], ("scan", "seq"), serve(4 * j)) for j in range(2)]
    else:
        columns = jnp.stack([w_query, w_key, w_value]).reshape(3, depth, sets, width)
        columns = jnp.transpose(columns, (2, 1, 0, 3)).reshape(sets, depth, 3 * width)
        columns = jnp.repeat(columns, group, axis=0)
        here = lax.all_to_all(
            columns, "seq", split_axis=0, concat_axis=0, tiled=True, axis_index_groups=same_core
        )
        there = lax.ppermute(here, "seq", swap)
        even = jnp.where(core == 0, here, there)
        odd = jnp.where(core == 0, there, here)
        weight = jnp.stack([even, odd], axis=1).reshape(D, 3 * width)
        out_weights = [lax.all_gather(w_out, "seq", axis=0, tiled=True)]

    load = load if packed else tokens
    length = load.shape[0] // 2
    forward = backward = load

    def spread(*shards):
        return [(shard, at) for shard in shards for at in (0, length)]

    state, others = (), []

    def advance(pieces, shards):
        nonlocal state, others
        q_all, kv_all, pair = project(
            [array for array, _ in pieces],
            tuple((at,) for _, at in pieces),
            gain,
            weight,
            width,
            chips,
            shards,
            tuple(held for _, held in others),
            state + tuple(other for other, _ in others),
        )
        state, others = (q_all, kv_all), []
        return pair

    def send(pair, shards):
        others.append((lax.ppermute(pair, "seq", swap), shards))

    arrived, shards = spread(load), (0,)
    for s in range(1, chips // 2 - 1):
        forward = lax.ppermute(forward, "seq", around(1))
        backward = lax.ppermute(backward, "seq", around(-1))
        if packed and s == 1:
            forward, backward, *moved = barrier((forward, backward, *moved))
        if packed and s == 2:
            blocks = keep(sent[0], *moved)
            twin_blocks = lax.ppermute(blocks, "scan", twins)
            joint = gather_blocks(
                [(blocks, 0), (blocks, 1), (twin_blocks, 0), (twin_blocks, 1)], False
            )
            weight = assemble(blocks, twin_blocks, lax.ppermute(joint, "seq", swap))
            forward, backward, weight = barrier((forward, backward, weight))
        arrived += spread(forward, backward)
        shards += (2 * s - 1, 2 * s)
    if packed:
        early = collect(arrived, depth // 2)
        early_twin = lax.ppermute(early, "scan", twins)
        weight, early_twin = barrier((weight, early_twin))
    pair = advance(arrived, shards)
    forward = lax.ppermute(forward, "seq", around(1))
    backward = lax.ppermute(backward, "seq", around(-1))
    forward, backward, pair, *state = barrier((forward, backward, pair, *state))
    state = tuple(state)
    final = (
        lax.ppermute(forward[:length], "seq", around(1)),
        lax.ppermute(backward[length:], "seq", around(-1)),
    )
    if packed:
        middle = collect(spread(forward, backward), depth // 2)
        middle_twin = lax.ppermute(middle, "scan", twins)
    near_shards = (chips - 3, chips - 2)
    near = advance(spread(forward, backward), near_shards)
    pair, near, *final = barrier((pair, near, *final))
    send(pair, shards)
    send(near, near_shards)
    held, others = others, []
    last = [(array, 0) for array in final]
    send(advance(last, (chips - 1,)), (chips - 1,))
    others = held + others
    if packed:
        late = collect(last, depth // 2)
        late_twin = lax.ppermute(late, "scan", twins)
    q_all, kv_all = state
    attended = attend(
        key_blocks.T,
        key_counts,
        q_all,
        kv_all,
        [other for other, _ in others],
        chips,
        group,
        heads,
        tuple(range(chips)),
        tuple(held for _, held in others),
    )[1:]
    if packed:
        first, middle_twin, late_twin = barrier((attended[0], middle_twin, late_twin))
        attended = [first, *attended[1:]]
        own_half = pair_rows(
            [(early, early_twin), (middle, middle_twin), (late, late_twin)], chips, True
        )
        other_half = lax.ppermute(own_half, "seq", swap)
        out_weights = [half.reshape(D // 2, D) for half in (own_half, other_half)]
    got = [attended[0]] + [lax.ppermute(attended[k], "seq", across(k)) for k in range(1, chips)]

    share = PROBES // ranks
    split = share % 16 == 0
    layer_out, *parts = tail(
        got,
        out_weights,
        tokens,
        probe_gain.reshape(1, D),
        probe_queries,
        chips,
        group,
        heads,
        split,
    )
    if split:
        mine, core_part, side_part, both_part = parts
        blocks = [
            mine,
            lax.ppermute(side_part, "seq", across(1)),
            lax.ppermute(both_part, "seq", [(i, i ^ 3) for i in range(ranks)]),
            lax.ppermute(core_part, "seq", swap),
        ]
        lines = deal(blocks, chips // 2)
        joined = [lines[0]] + [
            lax.ppermute(lines[k], "seq", across(2 * k)) for k in range(1, chips // 2)
        ]
        return layer_out, join(joined)
    rows = lax.all_to_all(
        parts[0].reshape(ranks, share, D + STATS), "seq", split_axis=0, concat_axis=0, tiled=True
    ).astype(F32)
    logs = rows[:, :, D : D + 3 * HEADS].reshape(ranks, share, 3, HEADS).sum(axis=2)
    factors = jnp.exp(logs - jnp.max(logs, axis=0, keepdims=True))
    factors = factors / jnp.sum(factors, axis=0, keepdims=True)
    probe_out = jnp.sum(jnp.repeat(factors, HEAD_DIM, axis=2) * rows[:, :, :D], axis=0)
    return layer_out, probe_out


def solution(mesh):
    return jax.shard_map(
        per_device,
        mesh=mesh,
        in_specs=(
            P(("scan", "seq"), None),
            P(),
            P("seq", None),
            P("seq", None),
            P("seq", None),
            P("seq", None),
            P(),
            P(),
            P("scan", None),
            P("scan"),
        ),
        out_specs=(P(("scan", "seq"), None), P(("scan", "seq"), None)),
        check_vma=False,
    )
```
